128 devices in a mesh: gx: 32 (over y, z, core), gy: 4 (over x).
Axes of the slice: x: 4, y: 4, z: 4, core: 2. Of those that a mesh axis runs over, the one named last changes fastest.
Arguments:
- right_side: float32 [3, 128, 64, 256], P(None, 'gx', 'gy'), may hold values from -45 to 45
- diag_blocks: float32 [9, 128, 64, 256], P(None, 'gx', 'gy'), may hold values from -1.2 to 1.8
- off_blocks: float32 [6, 9, 128, 64, 256], P(None, None, 'gx', 'gy'), may hold values from -0.25 to 0.16
- cell_inverse: float32 [9, 128, 64, 256], P(None, 'gx', 'gy'), may hold values from -0.4 to 0.85
- send_cells: int32 [128, 3200], P(('gx', 'gy')), may hold values from 0 to 16383, as said below
- recv_index: int32 [1024, 400], P(('gx', 'gy')), may hold values from 0 to 28799, as said below
- seg_count: int32 [1024], P(('gx', 'gy')), may hold values from 50 to 400, as said below
- span_inverse: float32 [25, 48, 49152], P(None, None, ('gx', 'gy')), may hold values from -0.24 to 1.2
- span_couple: float32 [25, 9, 1024], P(None, None, ('gx', 'gy')), may hold values from -3 to 3
Outputs:
- solution: float32 [3, 128, 64, 256], P(None, 'gx', 'gy')
- residual: float32 [3, 128, 64, 256], P(None, 'gx', 'gy')
The draws below stay inside these ranges and needn't reach their ends.
Inputs may be any that keep to these rules, and one draw needn't show every extreme that they name: `send_cells`: each row holds distinct local cells of its device. `recv_index`: over the live segments of one owner's wells the positions are distinct and name tiles inside the grid; entries of segments that are not live are arbitrary. `seg_count`: on one device in every draw all wells have 400 segments.
All inputs are finite; a program needn't handle non-finite values.
Results may differ from the reference program's by a relative error of at most 0.0001.
Values sent between devices are 32-bit elements; how exact they have to be, the bound alone decides.
A program may use at most 128 MiB of HBM per device.

```python
import math
import jax
import jax.numpy as jnp
from jax import lax

CX = 4
CY = 16
CZ = 256
WELLS_DEV = 8
MAXSEG = 400
SPAN = 16
NCHUNK = 25
SLOTS = 3200
WELLS = 1024
NX = 128
NY = 64
NZ = 256
N_GX = 32
N_GY = 4


def diagonal_mask(count):
    return jnp.arange(count) % 4 == 0


def draw_right_side(key, part):
    key_base, key_level = jax.random.split(jax.random.fold_in(key, 11))
    shape = (3, NX, NY, NZ)
    ramp = 1.0 + 2.0 * jnp.arange(NX, dtype=jnp.float32)[None, :, None, None] / max(NX - 1, 1)
    level = jnp.exp(jax.random.uniform(key_level, shape, jnp.float32, math.log(0.3), math.log(3.0)))
    base = jnp.clip(jax.random.normal(key_base, shape, jnp.float32), -5.0, 5.0)
    return base * ramp * level


def draw_diag_blocks(key, part):
    key_main, key_side = jax.random.split(jax.random.fold_in(key, 21))
    shape = (9, NX, NY, NZ)
    mask = diagonal_mask(9)[:, None, None, None]
    main = jax.random.uniform(key_main, shape, jnp.float32, 1.2, 1.8)
    side = 0.3 * jnp.clip(jax.random.normal(key_side, shape, jnp.float32), -4.0, 4.0)
    return jnp.where(mask, main, side)


def draw_off_blocks(key, part):
    key_main, key_side = jax.random.split(jax.random.fold_in(key, 31))
    shape = (6, 9, NX, NY, NZ)
    mask = diagonal_mask(9)[None, :, None, None, None]
    main = -jnp.exp(jax.random.uniform(key_main, shape, jnp.float32, math.log(0.05), math.log(0.25)))
    side = 0.04 * jnp.clip(jax.random.normal(key_side, shape, jnp.float32), -4.0, 4.0)
    return jnp.where(mask, main, side)


def draw_cell_inverse(key, part):
    key_main, key_side = jax.random.split(jax.random.fold_in(key, 41))
    shape = (9, NX, NY, NZ)
    mask = diagonal_mask(9)[:, None, None, None]
    main = jax.random.uniform(key_main, shape, jnp.float32, 0.55, 0.85)
    side = 0.1 * jnp.clip(jax.random.normal(key_side, shape, jnp.float32), -4.0, 4.0)
    return jnp.where(mask, main, side)


def draw_span_inverse(key, part):
    key_main, key_side = jax.random.split(jax.random.fold_in(key, 51))
    width = 3 * SPAN
    shape = (NCHUNK, width, WELLS * width)
    mask = (jnp.arange(width)[:, None] == jnp.arange(WELLS * width)[None, :] % width)[None]
    main = jax.random.uniform(key_main, shape, jnp.float32, 0.6, 1.2)
    side = 0.06 * jnp.clip(jax.random.normal(key_side, shape, jnp.float32), -4.0, 4.0)
    return jnp.where(mask, main, side)


def well_layout(key):
    base = jax.random.fold_in(key, 4242)
    keys = jax.random.split(base, 7)
    devices = N_GX * N_GY
    half = MAXSEG // 2
    device = jnp.arange(devices, dtype=jnp.int32)
    grid_x = device // N_GY
    grid_y = device % N_GY
    counts = jax.random.randint(keys[0], (devices, WELLS_DEV), MAXSEG // 4, MAXSEG + 1)
    full_x = jax.random.randint(keys[1], (), 1, N_GX - 1)
    full_y = jax.random.randint(keys[2], (), 1, N_GY - 1)
    near = (jnp.abs(grid_x - full_x) <= 1) & (jnp.abs(grid_y - full_y) <= 1)
    counts = jnp.where(near[:, None], MAXSEG, counts)
    phase = jax.random.randint(keys[3], (devices,), 0, 8)
    well = jnp.arange(WELLS_DEV, dtype=jnp.int32)
    heading = (well[None, :] + phase[:, None]) % 8
    step_x = jnp.take(jnp.array([-1, -1, -1, 0, 0, 1, 1, 1], jnp.int32), heading)
    step_y = jnp.take(jnp.array([-1, 0, 1, -1, 1, -1, 0, 1], jnp.int32), heading)
    host_x = grid_x[:, None] + step_x
    host_y = grid_y[:, None] + step_y
    inside = (host_x >= 0) & (host_x < N_GX) & (host_y >= 0) & (host_y < N_GY)
    tail = counts // 2
    head = counts - tail
    segs = jnp.where(inside, counts, head)
    place = (step_x + 1) * 3 + (step_y + 1)
    region = 8 * (well[None, :] // 8) + heading
    position = jnp.arange(MAXSEG, dtype=jnp.int32)[None, None, :]
    head_pos = 4 * SLOTS + well[None, :, None] * MAXSEG + position
    tail_pos = place[:, :, None] * SLOTS + region[:, :, None] * MAXSEG + half + position - head[:, :, None]
    live = position < segs[:, :, None]
    spare = jax.random.randint(keys[4], (devices, WELLS_DEV, MAXSEG), 0, 9 * SLOTS)
    index = jnp.where(position < head[:, :, None], head_pos, jnp.where(live, tail_pos, spare))
    columns = jax.vmap(lambda one_key: jax.random.permutation(one_key, CX * CY)[:2 * WELLS_DEV])(jax.random.split(keys[5], devices))
    depth = jax.random.randint(keys[6], (devices, 2 * WELLS_DEV), 0, CZ - half + 1)
    start = (columns * CZ + depth).reshape(devices, 2, WELLS_DEV).transpose(0, 2, 1)
    cells = start[:, :, :, None] + jnp.arange(half, dtype=jnp.int32)[None, None, None, :]
    return (segs.reshape(WELLS).astype(jnp.int32), index.reshape(WELLS, MAXSEG).astype(jnp.int32), cells.reshape(devices, SLOTS).astype(jnp.int32))


def draw_seg_count(key, part):
    return well_layout(key)[0]


def draw_recv_index(key, part):
    return well_layout(key)[1]


def draw_send_cells(key, part):
    return well_layout(key)[2]


def block_scale(rng, extent, cuts, low, top_value):
    def one(dim, blocks):
        steps = jax.random.uniform(jax.random.fold_in(jax.random.fold_in(rng, 6), dim), (blocks,), jnp.float32, low / len(cuts), top_value / len(cuts))
        return jnp.repeat(jnp.exp(steps), extent[dim] // blocks).reshape((-1,) + (1,) * (len(extent) - dim - 1))

    factor_of = one(*cuts[0])
    for cut in cuts[1:]:
        factor_of = factor_of * one(*cut)
    return factor_of


def normal_values(own_key, dims, scale, most, shards=(), held_as=jnp.bfloat16):
    result = scale * jax.random.normal(own_key, dims, jnp.float32)
    if shards:
        result = result * block_scale(own_key, dims, shards, -0.22, 0.18)
    return jnp.clip(result, -most, most).astype(held_as)


def setup_inputs(seed: int = 0) -> dict:
    splits = jax.random.split(jax.random.key(seed), 10)
    return {
        "right_side": draw_right_side(jax.random.fold_in(splits[9], 71), 0),
        "diag_blocks": draw_diag_blocks(jax.random.fold_in(splits[9], 71), 0),
        "off_blocks": draw_off_blocks(jax.random.fold_in(splits[9], 71), 0),
        "cell_inverse": draw_cell_inverse(jax.random.fold_in(splits[9], 71), 0),
        "send_cells": draw_send_cells(jax.random.fold_in(splits[9], 71), 0),
        "recv_index": draw_recv_index(jax.random.fold_in(splits[9], 71), 0),
        "seg_count": draw_seg_count(jax.random.fold_in(splits[9], 71), 0),
        "span_inverse": draw_span_inverse(jax.random.fold_in(splits[9], 71), 0),
        "span_couple": normal_values(splits[8], (NCHUNK, 9, WELLS), 0.5, 3.0, ((2, 128),), jnp.float32),
    }


def block_apply(matrix, vector):
    return jnp.stack([matrix[3 * a] * vector[0] + matrix[3 * a + 1] * vector[1] + matrix[3 * a + 2] * vector[2] for a in range(3)])

def apply_jacobian(field, diag_blocks, off_blocks):
    padded = jnp.pad(field, ((0, 0), (1, 1), (1, 1), (1, 1)))
    beside = [padded[:, :-2, 1:-1, 1:-1], padded[:, 2:, 1:-1, 1:-1], padded[:, 1:-1, :-2, 1:-1], padded[:, 1:-1, 2:, 1:-1], padded[:, 1:-1, 1:-1, :-2], padded[:, 1:-1, 1:-1, 2:]]
    total = block_apply(diag_blocks, field)
    for face in range(6):
        total = total + block_apply(off_blocks[face], beside[face])
    return total

def chain_solve(segments, span_inverse, span_couple):
    well_count = span_couple.shape[2]
    width = 3 * SPAN
    blocks = segments.reshape(3, well_count, NCHUNK, SPAN).transpose(2, 3, 0, 1).reshape(NCHUNK, width, well_count)
    inverse = span_inverse.reshape(NCHUNK, width, well_count, width)

    def advance(carry, packed):
        block_rhs, block_inverse, couple = packed
        first = block_rhs[:3] - block_apply(couple, carry)
        block_rhs = jnp.concatenate([first, block_rhs[3:]], axis=0)
        solved = lax.optimization_barrier(jnp.sum(block_inverse * block_rhs[:, :, None], axis=0)).T
        return (solved[width - 3:], solved)
    start = jnp.zeros((3, well_count), jnp.float32)
    _, solved = lax.scan(advance, start, (blocks, inverse, span_couple))
    return solved.reshape(NCHUNK, SPAN, 3, well_count).transpose(2, 3, 0, 1).reshape(3, well_count * MAXSEG)

def to_devices(field):
    count = field.shape[0]
    parts = field.reshape(count, N_GX, CX, N_GY, CY, NZ).transpose(0, 1, 3, 2, 4, 5)
    return parts.reshape(count, N_GX * N_GY, CX * CY * NZ)

def from_devices(parts):
    count = parts.shape[0]
    return parts.reshape(count, N_GX, N_GY, CX, CY, NZ).transpose(0, 1, 3, 2, 4, 5).reshape(count, NX, NY, NZ)

def neighbourhood(sent):
    count = sent.shape[0]
    grid = sent.reshape(count, N_GX, N_GY, SLOTS)
    padded = jnp.pad(grid, ((0, 0), (1, 1), (1, 1), (0, 0)))
    pieces = [padded[:, 1 + a:1 + a + N_GX, 1 + b:1 + b + N_GY] for a in (-1, 0, 1) for b in (-1, 0, 1)]
    return jnp.stack(pieces, axis=3).reshape(count, N_GX * N_GY, 9 * SLOTS)

def give_back(slots):
    count = slots.shape[0]
    grid = slots.reshape(count, N_GX, N_GY, 9, SLOTS)
    padded = jnp.pad(grid, ((0, 0), (1, 1), (1, 1), (0, 0), (0, 0)))
    total = jnp.zeros((count, N_GX, N_GY, SLOTS), jnp.float32)
    for a in (-1, 0, 1):
        for b in (-1, 0, 1):
            place = (1 - a) * 3 + (1 - b)
            total = total + padded[:, 1 + a:1 + a + N_GX, 1 + b:1 + b + N_GY, place]
    return total.reshape(count, N_GX * N_GY, SLOTS)

def least_squares(top_first, sub_first, top_second, mid_second, sub_second, beta):
    gram_first = top_first * top_first + sub_first * sub_first
    gram_cross = top_first * top_second + sub_first * mid_second
    gram_second = top_second * top_second + mid_second * mid_second + sub_second * sub_second
    determinant = gram_first * gram_second - gram_cross * gram_cross
    weight_one = (gram_second * beta * top_first - gram_cross * beta * top_second) / determinant
    weight_two = (gram_first * beta * top_second - gram_cross * beta * top_first) / determinant
    return (weight_one, weight_two)

def reference(right_side, diag_blocks, off_blocks, cell_inverse, send_cells, recv_index, seg_count, span_inverse, span_couple):
    devices = N_GX * N_GY
    cell_blocks = to_devices(diag_blocks)
    index = recv_index.reshape(devices, WELLS_DEV * MAXSEG)
    alive = (jnp.arange(MAXSEG)[None, :] < seg_count[:, None]).reshape(1, devices, WELLS_DEV * MAXSEG)
    sent_blocks = jnp.take_along_axis(cell_blocks, send_cells[None], axis=2)
    owner_blocks = jnp.take_along_axis(neighbourhood(sent_blocks), index[None], axis=2)

    def precondition(vector):
        parts = to_devices(vector)
        picked = jnp.take_along_axis(parts, send_cells[None], axis=2)
        arrived = jnp.take_along_axis(neighbourhood(picked), index[None], axis=2)
        segments = jnp.where(alive, block_apply(owner_blocks, arrived), 0.0)
        solved = chain_solve(segments.reshape(3, -1), span_inverse, span_couple).reshape(3, devices, -1)
        solved = jnp.where(alive, solved, 0.0)
        slots = jax.vmap(lambda where_to, values: jnp.zeros((3, 9 * SLOTS), jnp.float32).at[:, where_to].add(values), in_axes=(0, 1), out_axes=1)(index, solved)
        returned = give_back(slots)
        placed = jax.vmap(lambda cells, values: jnp.zeros((3, CX * CY * NZ), jnp.float32).at[:, cells].add(values), in_axes=(0, 1), out_axes=1)(send_cells, returned)
        return block_apply(cell_inverse, vector) + from_devices(placed)
    beta = jnp.sqrt(jnp.sum(right_side * right_side))
    basis = [right_side / beta]
    search = []
    entries = []
    for column in range(2):
        direction = precondition(basis[column])
        search.append(direction)
        image = apply_jacobian(direction, diag_blocks, off_blocks)
        coeffs = []
        for vector in basis:
            coeff = jnp.sum(image * vector)
            image = image - coeff * vector
            coeffs.append(coeff)
        size = jnp.sqrt(jnp.sum(image * image))
        entries.append((coeffs, size))
        basis.append(image / size)
    top_first, sub_first = (entries[0][0][0], entries[0][1])
    top_second, mid_second, sub_second = (entries[1][0][0], entries[1][0][1], entries[1][1])
    weight_one, weight_two = least_squares(top_first, sub_first, top_second, mid_second, sub_second, beta)
    solution = weight_one * search[0] + weight_two * search[1]
    residual = (beta - top_first * weight_one - top_second * weight_two) * basis[0] - (sub_first * weight_one + mid_second * weight_two) * basis[1] - sub_second * weight_two * basis[2]
    return (solution, residual)
```

```python
import functools

import jax
import jax.numpy as jnp
import numpy as np
from jax import lax
from jax.experimental import pallas as pl
from jax.experimental.pallas import tpu as pltpu
from jax.sharding import PartitionSpec as P

CX, CY, CZ = 4, 16, 256
WELLS = 8
MAXSEG = 400
SPAN = 16
NCHUNK = 25
WIDTH = 3 * SPAN
LANES = WELLS * WIDTH
ROWS = 25
MESH = pl.DeviceIdType.MESH
F32, BF16, I32 = jnp.float32, jnp.bfloat16, jnp.int32
NEAR = [(a, b) for a in (-1, 0, 1) for b in (-1, 0, 1)]
ORDER = [7, 1, 3, 5, 6, 8, 0, 2]


def expand_matrix():
    row = np.arange(9 * WELLS)
    lane = np.arange(3 * LANES)
    same = (row[:, None] // WELLS % 3 == lane[None] // LANES) & (
        row[:, None] % WELLS == lane[None] % LANES // WIDTH
    )
    return same.astype(np.float32)


def permute_matrix():
    lane = np.arange(LANES)
    well, segment, part = lane // WIDTH, lane % WIDTH // 3, lane % 3
    goal = part * 128 + well * SPAN + segment
    return (goal[:, None] == lane[None]).astype(np.float32)


def split3(x):
    first = x.astype(BF16).astype(F32)
    rest = x - first
    second = rest.astype(BF16).astype(F32)
    return first, second, rest - second


def lane_pick(row, lane):
    spread = jnp.broadcast_to(row, lane.shape)
    return jnp.take_along_axis(spread, lane, axis=1, mode="promise_in_bounds")


def kernel(
    n_gx,
    n_gy,
    rhs,
    diag,
    off_hbm,
    cinv_hbm,
    send,
    recv,
    seg_count,
    ginv_hbm,
    couple,
    expand,
    permute,
    sol,
    res,
    off,
    cinv,
    ginv,
    field,
    u,
    zp,
    ystage,
    yhalo,
    pool,
    slots,
    back,
    ret,
    cell,
    seg_row,
    seg_lane,
    inv_row,
    inv_lane,
    cell_row,
    cell_lane,
    spread,
    y0,
    yp,
    chain,
    ends,
    ytab,
    cpad,
    ar1,
    ar2,
    load_sem,
    fwd_send,
    fwd_recv,
    back_send,
    back_recv,
    halo_send,
    halo_recv,
    ar1_send,
    ar1_recv,
    ar2_send,
    ar2_recv,
):
    ix = lax.axis_index("gx")
    iy = lax.axis_index("gy")
    core = lax.rem(ix, 2)
    chip = lax.div(ix, 2)
    chips = n_gx // 2
    near = 2 * n_gy

    loads = [
        pltpu.make_async_copy(cinv_hbm, cinv, load_sem.at[0]),
        pltpu.make_async_copy(off_hbm, off, load_sem.at[1]),
    ] + [
        pltpu.make_async_copy(
            ginv_hbm.at[:, j * 128 : j * 128 + 128], ginv.at[j], load_sem.at[2 + j]
        )
        for j in range(3)
    ]
    for load in loads:
        load.start()

    def exists(q):
        a, b = NEAR[q]
        good = True
        if a < 0:
            good = ix > 0
        elif a > 0:
            good = ix < n_gx - 1
        if b < 0:
            good = good & (iy > 0)
        elif b > 0:
            good = good & (iy < n_gy - 1)
        return good

    def device(q):
        return (ix + NEAR[q][0], iy + NEAR[q][1])

    def near_device(d):
        place = lax.rem(core * n_gy + iy + d, near)
        return (chip * 2 + lax.div(place, n_gy), lax.rem(place, n_gy))

    def far_device(d):
        return (lax.rem(chip + d, chips) * 2 + core, iy)

    barrier = pltpu.get_barrier_semaphore()
    for q in ORDER:

        @pl.when(exists(q))
        def _(q=q):
            pl.semaphore_signal(barrier, inc=1, device_id=device(q), device_id_type=MESH)

    for d in range(1, near):
        pl.semaphore_signal(barrier, inc=1, device_id=near_device(d), device_id_type=MESH)
    for d in range(1, chips):
        pl.semaphore_signal(barrier, inc=1, device_id=far_device(d), device_id_type=MESH)

    def present(edge):
        return jnp.where(edge, 1, 0)

    across_x = 1 + present(ix > 0) + present(ix < n_gx - 1)
    across_y = 1 + present(iy > 0) + present(iy < n_gy - 1)
    greeted = across_x * across_y - 1 + (near - 1) + (chips - 1)

    def fwd_copy(it, q):
        return pltpu.make_async_remote_copy(
            src_ref=pool.at[it, 4],
            dst_ref=pool.at[it, 8 - q],
            send_sem=fwd_send.at[it, q],
            recv_sem=fwd_recv.at[it, 8 - q],
            device_id=device(q),
            device_id_type=MESH,
        )

    def back_copy(it, q):
        return pltpu.make_async_remote_copy(
            src_ref=slots.at[it, q],
            dst_ref=back.at[it, 8 - q],
            send_sem=back_send.at[it, q],
            recv_sem=back_recv.at[it, 8 - q],
            device_id=device(q),
            device_id_type=MESH,
        )

    side_place = [1, 7, 3, 5]

    def halo_copy(it, side):
        if side < 2:
            src = zp.at[it, 1 if side == 0 else CX]
            dst = zp.at[it, CX + 1 if side == 0 else 0]
        else:
            src = ystage.at[it, side - 2]
            dst = yhalo.at[it, 3 - side]
        other = side ^ 1
        return pltpu.make_async_remote_copy(
            src_ref=src,
            dst_ref=dst,
            send_sem=halo_send.at[it, side],
            recv_sem=halo_recv.at[it, other],
            device_id=device(side_place[side]),
            device_id_type=MESH,
        )

    def near_copy(i, d):
        return pltpu.make_async_remote_copy(
            src_ref=ar1.at[i, 0],
            dst_ref=ar1.at[i, d],
            send_sem=ar1_send.at[i, d],
            recv_sem=ar1_recv.at[i, d],
            device_id=near_device(d),
            device_id_type=MESH,
        )

    def far_copy(i, d):
        return pltpu.make_async_remote_copy(
            src_ref=ar2.at[i, 0],
            dst_ref=ar2.at[i, d],
            send_sem=ar2_send.at[i, d],
            recv_sem=ar2_recv.at[i, d],
            device_id=far_device(d),
            device_id_type=MESH,
        )

    def send_near(i):
        for d in range(1, near):
            near_copy(i, d).start()

    def pass_on(i):
        total = ar1[i, 0]
        for d in range(1, near):
            near_copy(i, d).wait_recv()
            total = total + ar1[i, d]
        ar2[i, 0] = total
        for d in range(1, chips):
            far_copy(i, d).start()

    def collect(i):
        total = ar2[i, 0]
        for d in range(1, chips):
            far_copy(i, d).wait_recv()
            total = total + ar2[i, d]
        return jnp.sum(total, axis=1, keepdims=True)

    for c in range(ROWS):
        cell[c : c + 1, :] = send[:, c * 128 : (c + 1) * 128]

    field[0] = rhs[...]

    def forward(it):
        for a in range(3):
            total = diag[3 * a] * field[it, 0]
            total = total + diag[3 * a + 1] * field[it, 1]
            total = total + diag[3 * a + 2] * field[it, 2]
            total = total.reshape(CX * CY, CZ)
            u[a, 0] = total[:, :128]
            u[a, 1] = total[:, 128:]
        where = cell[...]
        high = where >> 7
        lane = where & 127

        def step(r, got):
            got = list(got)
            for half in range(2):
                match = high == 2 * r + half
                for a in range(3):
                    row = u[a, half, pl.ds(r, 1), :]
                    got[a] = jnp.where(match, lane_pick(row, lane), got[a])
            return tuple(got)

        none = jnp.zeros((ROWS, 128), F32)
        got = lax.fori_loop(0, CX * CY, step, (none, none, none), unroll=2)
        for a in range(3):
            pool[it, 4, a] = got[a]

    def send_forward(it):
        for q in ORDER:

            @pl.when(exists(q))
            def _(q=q):
                fwd_copy(it, q).start()

    def setup():
        sub64 = lax.broadcasted_iota(I32, (CX * CY, 640), 0)
        sub256 = lax.broadcasted_iota(I32, (CZ, 640), 0)
        lanes = lax.broadcasted_iota(I32, (1, 640), 1)
        total = jnp.zeros((2 * CX * CY, CZ), F32)
        for m in range(5):
            where = send[:, m * 640 : m * 640 + 640]
            slot = lanes + m * 640
            hit = sub64 == (where >> 8)
            row = jnp.where(hit, ((slot >> 7) + 1).astype(F32), 0.0)
            lane = jnp.where(hit, (slot & 127).astype(F32), 0.0)
            left = jnp.concatenate([row, lane], axis=0).astype(BF16)
            right = jnp.where(sub256 == (where & 255), 1.0, 0.0).astype(BF16)
            total = total + lax.dot_general(
                left, right, (((1,), (1,)), ((), ())), preferred_element_type=F32
            )
        cell_row[...] = total[: CX * CY].astype(I32) - 1
        cell_lane[...] = total[CX * CY :].astype(I32)

        seg_lane[...] = jnp.zeros(seg_lane.shape, I32)
        seg_lane[:, :MAXSEG] = recv[...]
        position = seg_lane[...]
        well = lax.broadcasted_iota(I32, (WELLS, 512), 0)
        segment = lax.broadcasted_iota(I32, (WELLS, 512), 1)
        count = jnp.zeros((WELLS, 512), I32)
        for w in range(WELLS):
            count = jnp.where(well == w, seg_count[w], count)
        live = (segment < count) & (segment < MAXSEG)
        high = position >> 7
        seg_row[...] = jnp.where(live, high, -1)
        seg_lane[...] = position & 127

        sub288 = lax.broadcasted_iota(I32, (9 * 32, 512), 0)
        sub128 = lax.broadcasted_iota(I32, (128, 512), 0)
        along = lax.broadcasted_iota(I32, (1, 512), 1)
        total = jnp.zeros((2 * 9 * 32, 128), F32)
        for w in range(WELLS):
            high = seg_row[w : w + 1, :]
            slab = (high * 1311) >> 15
            goal = jnp.where(high < 0, -1, high + 7 * slab)
            hit = sub288 == goal
            row = jnp.where(hit, ((along >> 4) + 1).astype(F32), 0.0)
            lane = jnp.where(hit, ((along & 15) + w * SPAN).astype(F32), 0.0)
            left = jnp.concatenate([row, lane], axis=0).astype(BF16)
            right = jnp.where(sub128 == seg_lane[w : w + 1, :], 1.0, 0.0).astype(BF16)
            total = total + lax.dot_general(
                left, right, (((1,), (1,)), ((), ())), preferred_element_type=F32
            )
        inv_row[...] = total[: 9 * 32].astype(I32) - 1
        inv_lane[...] = total[9 * 32 :].astype(I32)

        cpad[...] = jnp.zeros(cpad.shape, F32)
        for c in range(NCHUNK):
            cpad[16 * c : 16 * c + 9, 0:WELLS] = couple[c]
        for j in range(3):
            loads[2 + j].wait()
        y0[...] = jnp.zeros(y0.shape, F32)
        group = lax.broadcasted_iota(I32, (NCHUNK, 128), 1) >> 4
        firsts = []
        for k in range(3):
            for j in range(3):
                y0[j, 0:NCHUNK] = ginv[j, pl.ds(k, NCHUNK, stride=WIDTH), :]
            firsts.append(permuted())
        pairs = [
            jnp.take_along_axis(
                cpad[pl.ds(kb, NCHUNK, stride=16), :], group, axis=1, mode="promise_in_bounds"
            )
            for kb in range(9)
        ]
        for a in range(3):
            for b in range(3):
                total = firsts[0][:NCHUNK, a * 128 : a * 128 + 128] * pairs[b]
                for k in (1, 2):
                    total = total + firsts[k][:NCHUNK, a * 128 : a * 128 + 128] * pairs[3 * k + b]
                chain[3 * a + b] = total
        for b in range(3):
            ends[b, 0:8] = jnp.zeros((8, 128), F32)

    def permuted():
        rows = jnp.concatenate([y0[j] for j in range(3)], axis=1)
        parts = jnp.concatenate(split3(rows), axis=0).astype(BF16)
        moved = jnp.dot(parts, permute[...], preferred_element_type=F32)
        return moved[0:32] + moved[32:64] + moved[64:96]

    def wells(it):
        row_of = seg_row[...]
        lane_of = seg_lane[...]
        rows4 = [row_of[:, j * 128 : j * 128 + 128] for j in range(4)]
        lanes4 = [lane_of[:, j * 128 : j * 128 + 128] for j in range(4)]
        none = jnp.zeros((WELLS, 128), F32)
        got = tuple([none] * 12)
        for q in [4] + ORDER:
            if q != 4:

                @pl.when(exists(q))
                def _(q=q):
                    fwd_copy(it, 8 - q).wait_recv()

            def step(r, got, q=q):
                got = list(got)
                match = [rows4[j] == q * ROWS + r for j in range(4)]
                for a in range(3):
                    row = pool[it, q, a, pl.ds(r, 1), :]
                    for j in range(4):
                        got[4 * a + j] = jnp.where(
                            match[j], lane_pick(row, lanes4[j]), got[4 * a + j]
                        )
                return tuple(got)

            got = lax.fori_loop(0, ROWS, step, got, unroll=5)
        parts = [split3(jnp.concatenate(got[4 * a : 4 * a + 4], axis=1)) for a in range(3)]
        stack = jnp.concatenate([parts[a][s] for s in range(3) for a in range(3)], axis=0)
        turned = stack.T.astype(BF16)[:MAXSEG]
        spread[...] = jnp.dot(turned, expand[...], preferred_element_type=F32)

        def block(c, carry):
            for j in range(3):
                total = None
                for a in range(3):
                    g = ginv[j, pl.ds(c * WIDTH + a, SPAN, stride=3), :]
                    at = pl.ds(pl.multiple_of(c * SPAN, SPAN), SPAN)
                    r = spread[at, a * LANES + j * 128 : a * LANES + j * 128 + 128]
                    total = g * r if total is None else total + g * r
                y0[j, pl.ds(c, 1), :] = jnp.sum(total, axis=0, keepdims=True)
            return carry

        lax.fori_loop(0, NCHUNK, block, 0, unroll=5)
        moved = permuted()
        for a in range(3):
            yp[a] = moved[:, a * 128 : a * 128 + 128]

        def link(c, last):
            new = []
            for a in range(3):
                value = yp[a, pl.ds(c, 1), :]
                for b in range(3):
                    value = value - chain[3 * a + b, pl.ds(c, 1), :] * last[b]
                new.append(value)
            for a in range(3):
                ends[a, pl.ds(c + 1, 1), :] = new[a]
            return tuple(new)

        lax.fori_loop(0, NCHUNK, link, tuple([jnp.zeros((1, 128), F32)] * 3), unroll=5)
        last_lane = lax.broadcasted_iota(I32, (NCHUNK, 128), 1) | 15
        before = [
            jnp.take_along_axis(
                ends[b, 0:NCHUNK, :], last_lane, axis=1, mode="promise_in_bounds"
            )
            for b in range(3)
        ]
        for a in range(3):
            value = yp[a, 0:NCHUNK]
            for b in range(3):
                value = value - chain[3 * a + b] * before[b]
            ytab[a] = value

        for q in ORDER + [4]:
            row_at = inv_row[q * 32 : q * 32 + ROWS, :]
            lane_at = inv_lane[q * 32 : q * 32 + ROWS, :]

            def step(r, got, row_at=row_at, lane_at=lane_at):
                match = row_at == r
                return tuple(
                    jnp.where(match, lane_pick(ytab[a, pl.ds(r, 1), :], lane_at), got[a])
                    for a in range(3)
                )

            none = jnp.zeros((ROWS, 128), F32)
            got = lax.fori_loop(0, ROWS, step, (none, none, none), unroll=5)
            for a in range(3):
                slots[it, q, a] = got[a]
            if q != 4:

                @pl.when(exists(q))
                def _(q=q):
                    back_copy(it, q).start()

    def backward(it):
        ret[...] = slots[it, 4]
        for q in ORDER:

            @pl.when(exists(q))
            def _(q=q):
                back_copy(it, 8 - q).wait_recv()
                ret[...] = ret[...] + back[it, q]

        def plane(x):
            row_at = cell_row[x * CY : x * CY + CY, :]
            lane_at = cell_lane[x * CY : x * CY + CY, :]
            row_at = [row_at[:, :128], row_at[:, 128:]]
            lane_at = [lane_at[:, :128], lane_at[:, 128:]]

            def step(r, got):
                got = list(got)
                match = [row_at[h] == r for h in range(2)]
                for a in range(3):
                    row = ret[a, pl.ds(r, 1), :]
                    for h in range(2):
                        got[2 * a + h] = jnp.where(
                            match[h], lane_pick(row, lane_at[h]), got[2 * a + h]
                        )
                return tuple(got)

            none = jnp.zeros((CY, 128), F32)
            got = lax.fori_loop(0, ROWS, step, tuple([none] * 6), unroll=5)
            for a in range(3):
                value = jnp.concatenate([got[2 * a], got[2 * a + 1]], axis=1)
                for b in range(3):
                    value = value + cinv[3 * a + b, x] * field[it, b, x]
                zp[it, x + 1, a] = value
                ystage[it, 0, pl.ds(3 * x + a, 1), :] = value[0:1]
                ystage[it, 1, pl.ds(3 * x + a, 1), :] = value[CY - 1 : CY]

        for x in (0, 3, 1, 2):
            plane(x)
            if x == 0:
                start_halo(it, 0)
            if x == 3:
                start_halo(it, 1)
        start_halo(it, 2)
        start_halo(it, 3)

    def start_halo(it, side):
        @pl.when(exists(side_place[side]))
        def _():
            halo_copy(it, side).start()

    def jacobian(it):
        row = lax.broadcasted_iota(I32, (CY, CZ), 0)
        column = lax.broadcasted_iota(I32, (CY, CZ), 1)
        for x in range(CX):
            total = [None] * 3

            def add(blocks, value, b):
                for a in range(3):
                    term = blocks(3 * a + b) * value
                    total[a] = term if total[a] is None else total[a] + term

            for b in range(3):
                here = zp[it, x + 1, b]
                add(lambda e: diag[e, x], here, b)
                if x > 0:
                    add(lambda e: off[0, e, x], zp[it, x, b], b)
                if x < CX - 1:
                    add(lambda e: off[1, e, x], zp[it, x + 2, b], b)
                value = jnp.where(row > 0, pltpu.roll(here, 1, 0), 0.0)
                add(lambda e: off[2, e, x], value, b)
                value = jnp.where(row < CY - 1, pltpu.roll(here, CY - 1, 0), 0.0)
                add(lambda e: off[3, e, x], value, b)
                value = jnp.where(column > 0, pltpu.roll(here, 1, 1), 0.0)
                add(lambda e: off[4, e, x], value, b)
                value = jnp.where(column < CZ - 1, pltpu.roll(here, CZ - 1, 1), 0.0)
                add(lambda e: off[5, e, x], value, b)
            for a in range(3):
                field[it + 1, a, x] = total[a]

        for side in range(4):

            @pl.when(exists(side_place[side]))
            def _(side=side):
                halo_copy(it, side ^ 1).wait_recv()
                if side < 2:
                    x = 0 if side == 0 else CX - 1
                    plane = 0 if side == 0 else CX + 1
                    for a in range(3):
                        value = field[it + 1, a, x]
                        for b in range(3):
                            value = value + off[side, 3 * a + b, x] * zp[it, plane, b]
                        field[it + 1, a, x] = value
                else:
                    y = 0 if side == 2 else CY - 1
                    for x in range(CX):
                        for a in range(3):
                            value = field[it + 1, a, x, y : y + 1, :]
                            for b in range(3):
                                beside = yhalo[it, side - 2, 3 * x + b : 3 * x + b + 1, :]
                                value = value + off[side, 3 * a + b, x, y : y + 1, :] * beside
                            field[it + 1, a, x, y : y + 1, :] = value

    def dot_row(i, place, first, second):
        total = None
        for a in range(3):
            for x in range(CX):
                product = first(a, x) * second(a, x)
                total = product if total is None else total + product
        total = jnp.sum(total, axis=0, keepdims=True)
        ar1[i, 0, place : place + 1, :] = total[:, :128] + total[:, 128:]

    for i in range(2):
        ar1[i, 0] = jnp.zeros((8, 128), F32)

    r_of = lambda a, x: rhs[a, x]
    w1_of = lambda a, x: field[1, a, x]
    w2_of = lambda a, x: field[2, a, x]
    v2_of = lambda a, x: field[0, a, x]

    forward(0)
    pl.semaphore_wait(barrier, greeted)
    send_forward(0)
    setup()
    wells(0)
    loads[0].wait()
    backward(0)
    loads[1].wait()
    jacobian(0)
    forward(1)
    send_forward(1)
    dot_row(0, 0, r_of, r_of)
    dot_row(0, 1, w1_of, r_of)
    send_near(0)
    wells(1)
    pass_on(0)
    backward(1)
    jacobian(1)

    first = collect(0)
    square = first[0:1]
    along = first[1:2] / square
    for a in range(3):
        for x in range(CX):
            field[0, a, x] = field[1, a, x] - along * rhs[a, x]
            field[2, a, x] = field[2, a, x] - along * field[1, a, x]
    dot_row(1, 0, v2_of, v2_of)
    dot_row(1, 1, w2_of, r_of)
    dot_row(1, 2, w2_of, v2_of)
    dot_row(1, 3, w2_of, w2_of)
    dot_row(1, 4, v2_of, r_of)
    send_near(1)
    pass_on(1)
    second = collect(1)

    beta = jnp.sqrt(square)
    size = jnp.sqrt(second[0:1])
    top_first = along
    sub_first = size / beta
    top_second = second[1:2] / (size * beta)
    mid_second = second[2:3] / (size * size) - top_second * (second[4:5] / (size * beta))
    gram_first = top_first * top_first + sub_first * sub_first
    gram_cross = top_first * top_second + sub_first * mid_second
    gram_second = second[3:4] / (size * size)
    determinant = gram_first * gram_second - gram_cross * gram_cross
    weight_one = (gram_second * beta * top_first - gram_cross * beta * top_second) / determinant
    weight_two = (gram_first * beta * top_second - gram_cross * beta * top_first) / determinant
    one = weight_one / beta
    two = weight_two / size
    mixed = one - two * along
    for a in range(3):
        for x in range(CX):
            sol[a, x] = mixed * zp[0, x + 1, a] + two * zp[1, x + 1, a]
            res[a, x] = rhs[a, x] - one * field[1, a, x] - two * field[2, a, x]

    for it in range(2):
        for q in ORDER:

            @pl.when(exists(q))
            def _(it=it, q=q):
                fwd_copy(it, q).wait_send()
                back_copy(it, q).wait_send()

        for side in range(4):

            @pl.when(exists(side_place[side]))
            def _(it=it, side=side):
                halo_copy(it, side).wait_send()

        for d in range(1, near):
            near_copy(it, d).wait_send()
        for d in range(1, chips):
            far_copy(it, d).wait_send()


def body(
    right_side,
    diag_blocks,
    off_blocks,
    cell_inverse,
    send_cells,
    recv_index,
    seg_count,
    span_inverse,
    span_couple,
):
    n_gx, n_gy = lax.axis_size("gx"), lax.axis_size("gy")
    vmem = pl.BlockSpec(memory_space=pltpu.VMEM)
    anywhere = pl.BlockSpec(memory_space=pl.ANY)
    smem = pl.BlockSpec(memory_space=pltpu.SMEM)
    shape = jax.ShapeDtypeStruct(right_side.shape, F32)
    dma = pltpu.SemaphoreType.DMA
    scratch = [
        pltpu.VMEM((6, 9, CX, CY, CZ), F32),
        pltpu.VMEM((9, CX, CY, CZ), F32),
        pltpu.VMEM((3, NCHUNK * WIDTH, 128), F32),
        pltpu.VMEM((3, 3, CX, CY, CZ), F32),
        pltpu.VMEM((3, 2, CX * CY, 128), F32),
        pltpu.VMEM((2, CX + 2, 3, CY, CZ), F32),
        pltpu.VMEM((2, 2, 12, CZ), F32),
        pltpu.VMEM((2, 2, 12, CZ), F32),
        pltpu.VMEM((2, 9, 3, ROWS, 128), F32),
        pltpu.VMEM((2, 9, 3, ROWS, 128), F32),
        pltpu.VMEM((2, 9, 3, ROWS, 128), F32),
        pltpu.VMEM((3, ROWS, 128), F32),
        pltpu.VMEM((ROWS, 128), I32),
        pltpu.VMEM((WELLS, 512), I32),
        pltpu.VMEM((WELLS, 512), I32),
        pltpu.VMEM((9 * 32, 128), I32),
        pltpu.VMEM((9 * 32, 128), I32),
        pltpu.VMEM((CX * CY, CZ), I32),
        pltpu.VMEM((CX * CY, CZ), I32),
        pltpu.VMEM((MAXSEG, 3 * LANES), F32),
        pltpu.VMEM((3, 32, 128), F32),
        pltpu.VMEM((3, 32, 128), F32),
        pltpu.VMEM((9, NCHUNK, 128), F32),
        pltpu.VMEM((3, 32, 128), F32),
        pltpu.VMEM((3, NCHUNK, 128), F32),
        pltpu.VMEM((16 * NCHUNK, 128), F32),
        pltpu.VMEM((2, 2 * n_gy, 8, 128), F32),
        pltpu.VMEM((2, n_gx // 2, 8, 128), F32),
        dma((5,)),
        dma((2, 9)),
        dma((2, 9)),
        dma((2, 9)),
        dma((2, 9)),
        dma((2, 4)),
        dma((2, 4)),
        dma((2, 2 * n_gy)),
        dma((2, 2 * n_gy)),
        dma((2, n_gx // 2)),
        dma((2, n_gx // 2)),
    ]
    return pl.pallas_call(
        functools.partial(kernel, n_gx, n_gy),
        out_shape=(shape, shape),
        in_specs=[vmem, vmem, anywhere, anywhere, vmem, vmem, smem, anywhere, vmem, vmem, vmem],
        out_specs=(vmem, vmem),
        scratch_shapes=scratch,
        compiler_params=pltpu.CompilerParams(collective_id=0, has_side_effects=True),
        name="gmres",
    )(
        right_side,
        diag_blocks,
        off_blocks,
        cell_inverse,
        send_cells,
        recv_index,
        seg_count,
        span_inverse.reshape(NCHUNK * WIDTH, LANES),
        span_couple,
        jnp.asarray(expand_matrix(), BF16),
        jnp.asarray(permute_matrix(), BF16),
    )


def solution(mesh):
    return jax.shard_map(
        body,
        mesh=mesh,
        in_specs=(
            P(None, "gx", "gy", None),
            P(None, "gx", "gy", None),
            P(None, None, "gx", "gy", None),
            P(None, "gx", "gy", None),
            P(("gx", "gy"), None),
            P(("gx", "gy"), None),
            P(("gx", "gy")),
            P(None, None, ("gx", "gy")),
            P(None, None, ("gx", "gy")),
        ),
        out_specs=(P(None, "gx", "gy", None), P(None, "gx", "gy", None)),
        check_vma=False,
    )
```

```python
import functools

import jax
import jax.numpy as jnp
from jax import lax
from jax.experimental import pallas as pl
from jax.experimental.pallas import tpu as pltpu
from jax.sharding import PartitionSpec as P

CX, CY, CZ = 4, 16, 256
WELLS = 8
MAXSEG = 400
SPAN = 16
NCHUNK = 25
WIDTH = 3 * SPAN
LANES = WELLS * WIDTH
ROWS = 25
MESH = pl.DeviceIdType.MESH
F32, BF16, I32 = jnp.float32, jnp.bfloat16, jnp.int32
NEAR = [(a, b) for a in (-1, 0, 1) for b in (-1, 0, 1)]
ORDER = [7, 1, 3, 5, 6, 8, 0, 2]


def lane_pick(row, lane):
    numbers = lax.GatherDimensionNumbers(
        offset_dims=(),
        collapsed_slice_dims=(1,),
        start_index_map=(1,),
        operand_batching_dims=(0,),
        start_indices_batching_dims=(0,),
    )
    return lax.gather(
        jnp.broadcast_to(row, lane.shape),
        lane[..., None],
        numbers,
        slice_sizes=(1, 1),
        mode=lax.GatherScatterMode.PROMISE_IN_BOUNDS,
    )


def look_up(rows, lane, count, match, parts=4):
    totals = []
    for a in range(3):
        totals.append([None] * parts)
    for r in range(count):
        hit = match(r)
        for a in range(3):
            old = totals[a][r % parts]
            old = jnp.zeros(lane.shape, F32) if old is None else old
            totals[a][r % parts] = jnp.where(hit, lane_pick(rows(a, r), lane), old)
    return [functools.reduce(jnp.add, [t for t in totals[a] if t is not None]) for a in range(3)]


def kernel(
    n_gx,
    n_gy,
    rhs,
    diag,
    off_hbm,
    cinv_hbm,
    send,
    recv,
    seg_count,
    ginv_hbm,
    couple,
    sol,
    res,
    off,
    cinv,
    ginv,
    field,
    u,
    zp,
    ystage,
    yhalo,
    pool,
    slots,
    back,
    ret,
    cell,
    seg_row,
    seg_lane,
    inv_row,
    inv_lane,
    cell_row,
    cell_lane,
    spread,
    y0,
    yp,
    chain,
    ends,
    ytab,
    cpad,
    ar1,
    ar2,
    sums,
    load_sem,
    fwd_send,
    fwd_recv,
    back_send,
    back_recv,
    halo_send,
    halo_recv,
    ar1_send,
    ar1_recv,
    ar2_send,
    ar2_recv,
):
    ix = lax.axis_index("gx")
    iy = lax.axis_index("gy")
    core = lax.rem(ix, 2)
    chip = lax.div(ix, 2)
    chips = n_gx // 2
    near = 2 * n_gy

    loads = [
        pltpu.make_async_copy(cinv_hbm, cinv, load_sem.at[0]),
        pltpu.make_async_copy(off_hbm, off, load_sem.at[1]),
    ] + [
        pltpu.make_async_copy(
            ginv_hbm.at[:, j * 128 : j * 128 + 128], ginv.at[j], load_sem.at[2 + j]
        )
        for j in range(3)
    ]
    for load in loads:
        load.start()

    def exists(q):
        a, b = NEAR[q]
        good = True
        if a < 0:
            good = ix > 0
        elif a > 0:
            good = ix < n_gx - 1
        if b < 0:
            good = good & (iy > 0)
        elif b > 0:
            good = good & (iy < n_gy - 1)
        return good

    def device(q):
        if isinstance(q, int):
            return (ix + NEAR[q][0], iy + NEAR[q][1])
        return (ix + lax.div(q, 3) - 1, iy + lax.rem(q, 3) - 1)

    def exists_at(q):
        gx, gy = device(q)
        return (gx >= 0) & (gx < n_gx) & (gy >= 0) & (gy < n_gy) & (q != 4)

    def near_device(d):
        place = lax.rem(core * n_gy + iy + d, near)
        return (chip * 2 + lax.div(place, n_gy), lax.rem(place, n_gy))

    def far_device(d):
        return (lax.rem(chip + d, chips) * 2 + core, iy)

    barrier = pltpu.get_barrier_semaphore()
    for q in ORDER:

        @pl.when(exists(q))
        def _(q=q):
            pl.semaphore_signal(barrier, inc=1, device_id=device(q), device_id_type=MESH)

    for d in range(1, near):
        pl.semaphore_signal(barrier, inc=1, device_id=near_device(d), device_id_type=MESH)
    for d in range(1, chips):
        pl.semaphore_signal(barrier, inc=1, device_id=far_device(d), device_id_type=MESH)

    def present(edge):
        return jnp.where(edge, 1, 0)

    across_x = 1 + present(ix > 0) + present(ix < n_gx - 1)
    across_y = 1 + present(iy > 0) + present(iy < n_gy - 1)
    greeted = across_x * across_y - 1 + (near - 1) + (chips - 1)

    def fwd_copy(it, q):
        return pltpu.make_async_remote_copy(
            src_ref=pool.at[it, 4],
            dst_ref=pool.at[it, 8 - q],
            send_sem=fwd_send.at[it, q],
            recv_sem=fwd_recv.at[it, 8 - q],
            device_id=device(q),
            device_id_type=MESH,
        )

    def fwd_arrival(it, q):
        return pltpu.make_async_remote_copy(
            src_ref=pool.at[it, 4],
            dst_ref=pool.at[it, q],
            send_sem=fwd_send.at[it, 8 - q],
            recv_sem=fwd_recv.at[it, q],
            device_id=device(q),
            device_id_type=MESH,
        )

    def back_copy(it, q):
        return pltpu.make_async_remote_copy(
            src_ref=slots.at[it, q],
            dst_ref=back.at[it, 8 - q],
            send_sem=back_send.at[it, q],
            recv_sem=back_recv.at[it, 8 - q],
            device_id=device(q),
            device_id_type=MESH,
        )

    side_place = [1, 7, 3, 5]

    def halo_copy(it, side):
        if side < 2:
            src = zp.at[it, 1 if side == 0 else CX]
            dst = zp.at[it, CX + 1 if side == 0 else 0]
        else:
            src = ystage.at[it, side - 2]
            dst = yhalo.at[it, 3 - side]
        other = side ^ 1
        return pltpu.make_async_remote_copy(
            src_ref=src,
            dst_ref=dst,
            send_sem=halo_send.at[it, side],
            recv_sem=halo_recv.at[it, other],
            device_id=device(side_place[side]),
            device_id_type=MESH,
        )

    def near_copy(i, d):
        return pltpu.make_async_remote_copy(
            src_ref=ar1.at[i, 0],
            dst_ref=ar1.at[i, d],
            send_sem=ar1_send.at[i, d],
            recv_sem=ar1_recv.at[i, d],
            device_id=near_device(d),
            device_id_type=MESH,
        )

    def far_copy(i, d):
        return pltpu.make_async_remote_copy(
            src_ref=ar2.at[i, 0],
            dst_ref=ar2.at[i, d],
            send_sem=ar2_send.at[i, d],
            recv_sem=ar2_recv.at[i, d],
            device_id=far_device(d),
            device_id_type=MESH,
        )

    def sent(it, copy, count, place=lambda k: k):
        for k in range(count):
            if place(k) != 4:

                @pl.when(exists(place(k)))
                def _(k=k):
                    copy(it, k).wait_send()

    def sent_halo(it):
        sent(it, halo_copy, 4, lambda side: side_place[side])

    def sent_sums(i):
        for d in range(1, near):
            near_copy(i, d).wait_send()
        for d in range(1, chips):
            far_copy(i, d).wait_send()

    def send_near(i):
        for d in range(1, near):
            near_copy(i, d).start()

    def pass_on(i):
        total = ar1[i, 0]
        for d in range(1, near):
            near_copy(i, d).wait_recv()
            total = total + ar1[i, d]
        ar2[i, 0] = total
        for d in range(1, chips):
            far_copy(i, d).start()

    def collect(i):
        total = ar2[i, 0]
        for d in range(1, chips):
            far_copy(i, d).wait_recv()
            total = total + ar2[i, d]
        return total

    for c in range(ROWS):
        cell[c : c + 1, :] = send[:, c * 128 : (c + 1) * 128]

    field[0] = rhs[...]

    def forward(it):
        for a in range(3):
            total = diag[3 * a] * field[it, 0]
            total = total + diag[3 * a + 1] * field[it, 1]
            total = total + diag[3 * a + 2] * field[it, 2]
            u[a, 0] = total[:, :, :128]
            u[a, 1] = total[:, :, 128:]
        where = cell[...]
        high = where >> 7
        lane = where & 127
        sub = lax.broadcasted_iota(I32, (8, 128), 0)
        tiles = [slice(8 * i, 8 * i + 8) for i in range(3)]
        end_high = jnp.broadcast_to(high[24:25], (8, 128)) - 2 * sub
        end_lane = jnp.broadcast_to(lane[24:25], (8, 128))

        def step(g, got):
            got = list(got)
            for i, tile in enumerate(tiles):
                base = high[tile] - 64 * g
                new = look_up(
                    lambda a, r: u[a, r % 2, 2 * g + r // 32, r // 2 % 16 : r // 2 % 16 + 1, :],
                    lane[tile],
                    64,
                    lambda r: base == r,
                )
                for a in range(3):
                    got[3 * i + a] = got[3 * i + a] + new[a]
            base = end_high - 64 * g
            for r in range(0, 32, 8):
                for half in range(2):
                    match = base == 2 * r + half
                    for a in range(3):
                        here = u[a, half, 2 * g + r // 16, r % 16 : r % 16 + 8, :]
                        value = lane_pick(here, end_lane)
                        got[9 + a] = jnp.where(match, value, got[9 + a])
            return tuple(got)

        none = jnp.zeros((8, 128), F32)
        got = lax.fori_loop(0, CX // 2, step, tuple([none] * 12))
        for a in range(3):
            for i, tile in enumerate(tiles):
                pool[it, 4, a, tile] = got[3 * i + a]
            pool[it, 4, a, 24:25] = jnp.sum(got[9 + a], axis=0, keepdims=True)

    def send_forward(it):
        for q in ORDER:

            @pl.when(exists(q))
            def _(q=q):
                fwd_copy(it, q).start()

    def setup():
        total = jnp.zeros((CX * CY, 2 * CZ), F32)
        for start, width in ((0, 1024), (1024, 1024), (2048, 1024), (3072, 128)):
            where = send[:, start : start + width]
            slot = lax.broadcasted_iota(I32, (1, width), 1) + start
            left = lax.broadcasted_iota(I32, (CX * CY, width), 0) == (where >> 8)
            hit = lax.broadcasted_iota(I32, (CZ, width), 0) == (where & 255)
            row = jnp.where(hit, ((slot >> 7) + 1).astype(F32), 0.0)
            lane = jnp.where(hit, (slot & 127).astype(F32), 0.0)
            total = total + lax.dot_general(
                jnp.where(left, 1.0, 0.0).astype(BF16),
                jnp.concatenate([row, lane], axis=0).astype(BF16),
                (((1,), (1,)), ((), ())),
                preferred_element_type=F32,
            )
        cell_row[...] = total[:, :CZ].astype(I32).reshape(CX, CY, CZ) - 1
        cell_lane[...] = total[:, CZ:].astype(I32).reshape(CX, CY, CZ)

        seg_lane[...] = jnp.zeros(seg_lane.shape, I32)
        seg_lane[:, :MAXSEG] = recv[...]
        position = seg_lane[...]
        well = lax.broadcasted_iota(I32, (WELLS, 512), 0)
        segment = lax.broadcasted_iota(I32, (WELLS, 512), 1)
        count = jnp.zeros((WELLS, 512), I32)
        for w in range(WELLS):
            count = jnp.where(well == w, seg_count[w], count)
        live = (segment < count) & (segment < MAXSEG)
        high = position >> 7
        seg_row[...] = jnp.where(live, high, -1)
        seg_lane[...] = position & 127

        sub232 = lax.broadcasted_iota(I32, (232, 512), 0)
        sub128 = lax.broadcasted_iota(I32, (128, 512), 0)
        along = lax.broadcasted_iota(I32, (1, 512), 1)
        total = jnp.zeros((232, 256), F32)
        for w in range(WELLS):
            high = seg_row[w : w + 1, :]
            slab = (high * 1311) >> 15
            row_in = high - ROWS * slab
            goal = jnp.where(row_in == ROWS - 1, 9 * 24 + slab, 24 * slab + row_in)
            left = sub232 == jnp.where(high < 0, -1, goal)
            hit = sub128 == seg_lane[w : w + 1, :]
            row = jnp.where(hit, ((along >> 4) + 1).astype(F32), 0.0)
            lane = jnp.where(hit, ((along & 15) + w * SPAN).astype(F32), 0.0)
            total = total + lax.dot_general(
                jnp.where(left, 1.0, 0.0).astype(BF16),
                jnp.concatenate([row, lane], axis=0).astype(BF16),
                (((1,), (1,)), ((), ())),
                preferred_element_type=F32,
            )
        for q in range(9):
            inv_row[q] = total[24 * q : 24 * q + 24, :128].astype(I32) - 1
            inv_lane[q] = total[24 * q : 24 * q + 24, 128:].astype(I32)
        inv_row[9, 0:16] = total[216:232, :128].astype(I32) - 1
        inv_lane[9, 0:16] = total[216:232, 128:].astype(I32)

        for j in range(3):
            loads[2 + j].wait()
        y0[...] = jnp.zeros(y0.shape, F32)
        group = lax.broadcasted_iota(I32, (32, 128), 1) >> 4
        firsts = []
        for k in range(3):
            for j in range(3):
                y0[j, 0:NCHUNK] = ginv[j, pl.ds(k, NCHUNK, stride=WIDTH), :]
            firsts.append(permuted())
        pairs = []
        cpad[...] = jnp.zeros(cpad.shape, F32)
        for kb in range(9):
            cpad[0:WELLS, 0:NCHUNK] = couple[kb]
            pairs.append(lane_pick(cpad[...].T[0:32], group)[:NCHUNK])
        for a in range(3):
            for b in range(3):
                total = firsts[0][a][:NCHUNK] * pairs[b]
                for k in (1, 2):
                    total = total + firsts[k][a][:NCHUNK] * pairs[3 * k + b]
                chain[3 * a + b] = total
        for b in range(3):
            ends[b, 0:8] = jnp.zeros((8, 128), F32)

    def permuted():
        lane = lax.broadcasted_iota(I32, (8, 128), 1)
        result = []
        for a in range(3):
            source = (lane >> 4) * WIDTH + 3 * (lane & 15) + a
            tiles = [None] * 4
            for j in range(3):
                here = (source >> 7) == j
                for i in range(4):
                    value = lane_pick(y0[j, 8 * i : 8 * i + 8], source & 127)
                    tiles[i] = value if j == 0 else jnp.where(here, value, tiles[i])
            result.append(jnp.concatenate(tiles, axis=0))
        return result

    def wells(it):
        row_of = seg_row[...]
        lane_of = seg_lane[...]
        tiles = [slice(128 * i, 128 * i + 128) for i in range(3)]
        sub = lax.broadcasted_iota(I32, (8, 128), 0)
        along = lax.broadcasted_iota(I32, (8, 128), 1)
        mine = (along >> 4) == sub

        def one_row(values):
            value = lane_pick(values[:, 384:], along & 15)
            return jnp.sum(jnp.where(mine, value, 0), axis=0, keepdims=True)

        end_row = jnp.broadcast_to(one_row(row_of), (8, 128)) - sub
        end_lane = jnp.broadcast_to(one_row(lane_of), (8, 128))

        def take(q, got):
            got = list(got)
            for i, tile in enumerate(tiles):
                base = row_of[:, tile] - q * ROWS
                new = look_up(
                    lambda a, r: pool[it, q, a, r : r + 1, :],
                    lane_of[:, tile],
                    ROWS,
                    lambda r: base == r,
                )
                for a in range(3):
                    got[3 * i + a] = got[3 * i + a] + new[a]
            base = end_row - q * ROWS
            for r in range(0, 24, 8):
                match = base == r
                for a in range(3):
                    value = lane_pick(pool[it, q, a, r : r + 8, :], end_lane)
                    got[9 + a] = jnp.where(match, value, got[9 + a])
            match = (base == 24) & (sub == 0)
            for a in range(3):
                value = lane_pick(pool[it, q, a, 24:25, :], end_lane)
                got[9 + a] = jnp.where(match, value, got[9 + a])
            return tuple(got)

        def step(p, got):
            q = lax.rem(2 * p + 1, 5)
            for side in (q, 8 - q):

                @pl.when(exists_at(side))
                def _(side=side):
                    fwd_arrival(it, side).wait_recv()

            return take(8 - q, take(q, got))

        none = jnp.zeros((WELLS, 128), F32)
        got = take(4, tuple([none] * 12))
        got = list(lax.fori_loop(0, 4, step, got))
        for a in range(3):
            value = jnp.sum(got[9 + a], axis=0, keepdims=True)
            value = lane_pick(value, (sub * 16 + along) & 127)
            got[9 + a] = jnp.where(along < 16, value, 0.0)
        none = jnp.zeros((WELLS, 128), F32)
        for i in range(4):
            square = jnp.concatenate([got[3 * i + a] for a in range(3)] + [none] * 13, axis=0)
            spread[128 * i : 128 * i + 128] = square.T
        well = [(along + 128 * j) // WIDTH for j in range(3)]
        for j in range(3):
            totals = [None] * NCHUNK
            for a in range(3):
                for c in range(NCHUNK):
                    for at in (SPAN * c, SPAN * c + 8):
                        r = lane_pick(spread[at : at + 8], well[j] + 8 * a)
                        g = ginv[j, pl.ds(3 * at + a, 8, stride=3), :]
                        totals[c] = g * r if totals[c] is None else totals[c] + g * r
            for c in range(NCHUNK):
                y0[j, c : c + 1, :] = jnp.sum(totals[c], axis=0, keepdims=True)
        moved = permuted()
        for a in range(3):
            yp[a] = moved[a]

        def link(c, last):
            new = []
            for a in range(3):
                value = yp[a, pl.ds(c, 1), :]
                for b in range(3):
                    value = value - chain[3 * a + b, pl.ds(c, 1), :] * last[b]
                new.append(value)
            for a in range(3):
                ends[a, pl.ds(c + 1, 1), :] = new[a]
            return tuple(new)

        lax.fori_loop(0, NCHUNK, link, tuple([jnp.zeros((1, 128), F32)] * 3), unroll=5)
        last_lane = lax.broadcasted_iota(I32, (NCHUNK, 128), 1) | 15
        before = [lane_pick(ends[b, 0:NCHUNK, :], last_lane) for b in range(3)]
        for a in range(3):
            value = yp[a, 0:NCHUNK]
            for b in range(3):
                value = value - chain[3 * a + b] * before[b]
            ytab[a] = value

        def corrections(row_at, lane_at):
            return look_up(
                lambda a, r: ytab[a, r : r + 1, :], lane_at, ROWS, lambda r: row_at == r
            )

        for half in range(2):
            tile = slice(8 * half, 8 * half + 8)
            got = corrections(inv_row[9, tile], inv_lane[9, tile])
            for q in range(8 * half, min(9, 8 * half + 8)):
                for a in range(3):
                    slots[it, q, a, 24:25] = got[a][q - 8 * half : q - 8 * half + 1]

        def give(q):
            for i in range(3):
                tile = slice(8 * i, 8 * i + 8)
                got = corrections(inv_row[q, tile], inv_lane[q, tile])
                for a in range(3):
                    slots[it, q, a, tile] = got[a]

        def give_pair(t, carry):
            q = lax.rem(2 * (3 - t) + 1, 5)
            give(q)
            give(8 - q)
            for side in (q, 8 - q):

                @pl.when(exists_at(side))
                def _(side=side):
                    back_copy(it, side).start()

            return carry

        lax.fori_loop(0, 4, give_pair, 0)
        give(4)

    def backward(it):
        ret[...] = slots[it, 4]
        for q in ORDER:

            @pl.when(exists(q))
            def _(q=q):
                back_copy(it, 8 - q).wait_recv()
                ret[...] = ret[...] + back[it, q]

        def plane(x):
            for i in range(2):
                sides = []
                for half in range(2):
                    tile = (slice(8 * i, 8 * i + 8), slice(128 * half, 128 * half + 128))
                    row_at = cell_row[(x,) + tile]
                    lane_at = cell_lane[(x,) + tile]
                    got = look_up(
                        lambda a, r: ret[a, r : r + 1, :], lane_at, ROWS, lambda r: row_at == r
                    )
                    for a in range(3):
                        value = got[a]
                        for b in range(3):
                            value = value + cinv[(3 * a + b, x) + tile] * field[(it, b, x) + tile]
                        zp[(it, x + 1, a) + tile] = value
                        if i == 0:
                            ystage[it, 0, x, a : a + 1, tile[1]] = value[0:1]
                        else:
                            ystage[it, 1, x, a : a + 1, tile[1]] = value[7:8]

        def planes(t, carry):
            plane(t)
            plane(3 - t)

            @pl.when((t == 0) & exists(1))
            def _():
                halo_copy(it, 0).start()

            @pl.when((t == 0) & exists(7))
            def _():
                halo_copy(it, 1).start()

            return carry

        lax.fori_loop(0, 2, planes, 0)
        start_halo(it, 2)
        start_halo(it, 3)

    def start_halo(it, side):
        @pl.when(exists(side_place[side]))
        def _():
            halo_copy(it, side).start()

    def jacobian(it, between=lambda: None):
        row = lax.broadcasted_iota(I32, (CY, CZ), 0)
        column = lax.broadcasted_iota(I32, (CY, CZ), 1)
        for x in range(CX):
            total = [None] * 3

            def add(blocks, value, b):
                for a in range(3):
                    term = blocks(3 * a + b) * value
                    total[a] = term if total[a] is None else total[a] + term

            for b in range(3):
                here = zp[it, x + 1, b]
                add(lambda e: diag[e, x], here, b)
                if x > 0:
                    add(lambda e: off[0, e, x], zp[it, x, b], b)
                if x < CX - 1:
                    add(lambda e: off[1, e, x], zp[it, x + 2, b], b)
                value = jnp.where(row > 0, pltpu.roll(here, 1, 0), 0.0)
                add(lambda e: off[2, e, x], value, b)
                value = jnp.where(row < CY - 1, pltpu.roll(here, CY - 1, 0), 0.0)
                add(lambda e: off[3, e, x], value, b)
                value = jnp.where(column > 0, pltpu.roll(here, 1, 1), 0.0)
                add(lambda e: off[4, e, x], value, b)
                value = jnp.where(column < CZ - 1, pltpu.roll(here, CZ - 1, 1), 0.0)
                add(lambda e: off[5, e, x], value, b)
            for a in range(3):
                field[it + 1, a, x] = total[a]

        result = between()
        for side in range(4):

            @pl.when(exists(side_place[side]))
            def _(side=side):
                halo_copy(it, side ^ 1).wait_recv()
                if side < 2:
                    x = 0 if side == 0 else CX - 1
                    plane = 0 if side == 0 else CX + 1
                    for a in range(3):
                        value = field[it + 1, a, x]
                        for b in range(3):
                            value = value + off[side, 3 * a + b, x] * zp[it, plane, b]
                        field[it + 1, a, x] = value
                else:
                    y = 0 if side == 2 else CY - 1
                    for x in range(CX):
                        for a in range(3):
                            value = field[it + 1, a, x, y : y + 1, :]
                            for b in range(3):
                                beside = yhalo[it, side - 2, x, b : b + 1, :]
                                value = value + off[side, 3 * a + b, x, y : y + 1, :] * beside
                            field[it + 1, a, x, y : y + 1, :] = value
        return result

    def dot_row(place, first, second):
        total = None
        for a in range(3):
            for x in range(CX):
                product = first(a, x) * second(a, x)
                total = product if total is None else total + product
        total = jnp.sum(total, axis=0, keepdims=True)
        sums[place : place + 1, :] = total[:, :128] + total[:, 128:]

    def pack_sums(i):
        sub = lax.broadcasted_iota(I32, (8, 128), 0)
        along = lax.broadcasted_iota(I32, (8, 128), 1)
        total = jnp.sum(sums[...], axis=1, keepdims=True)
        ar1[i, 0] = jnp.sum(jnp.where(sub == along, total, 0.0), axis=0, keepdims=True)

    sums[...] = jnp.zeros((8, 128), F32)

    r_of = lambda a, x: rhs[a, x]
    w1_of = lambda a, x: field[1, a, x]
    w2_of = lambda a, x: field[2, a, x]
    v2_of = lambda a, x: field[0, a, x]

    forward(0)
    pl.semaphore_wait(barrier, greeted)
    send_forward(0)
    setup()
    wells(0)
    sent(0, fwd_copy, 9)
    loads[0].wait()
    backward(0)
    loads[1].wait()
    jacobian(0)
    forward(1)
    send_forward(1)
    dot_row(0, r_of, r_of)
    dot_row(1, w1_of, r_of)
    pack_sums(0)
    send_near(0)
    sent(0, back_copy, 9)
    sent_halo(0)
    wells(1)
    pass_on(0)
    sent(1, fwd_copy, 9)
    backward(1)

    def between():
        first = collect(0)
        square = first[:, 0:1]
        along = first[:, 1:2] / square
        for a in range(3):
            for x in range(CX):
                field[0, a, x] = field[1, a, x] - along * rhs[a, x]
        dot_row(0, v2_of, v2_of)
        dot_row(4, v2_of, r_of)
        return square, along

    square, along = jacobian(1, between)
    for a in range(3):
        for x in range(CX):
            field[2, a, x] = field[2, a, x] - along * field[1, a, x]
    dot_row(1, w2_of, r_of)
    dot_row(2, w2_of, v2_of)
    dot_row(3, w2_of, w2_of)
    pack_sums(1)
    send_near(1)
    sent(1, back_copy, 9)
    sent_halo(1)
    sent_sums(0)
    pass_on(1)
    second = collect(1)

    beta = jnp.sqrt(square)
    size = jnp.sqrt(second[:, 0:1])
    top_first = along
    sub_first = size / beta
    top_second = second[:, 1:2] / (size * beta)
    mid_second = second[:, 2:3] / (size * size) - top_second * (second[:, 4:5] / (size * beta))
    gram_first = top_first * top_first + sub_first * sub_first
    gram_cross = top_first * top_second + sub_first * mid_second
    gram_second = second[:, 3:4] / (size * size)
    determinant = gram_first * gram_second - gram_cross * gram_cross
    weight_one = (gram_second * beta * top_first - gram_cross * beta * top_second) / determinant
    weight_two = (gram_first * beta * top_second - gram_cross * beta * top_first) / determinant
    one = weight_one / beta
    two = weight_two / size
    mixed = one - two * along
    for a in range(3):
        for x in range(CX):
            sol[a, x] = mixed * zp[0, x + 1, a] + two * zp[1, x + 1, a]
            res[a, x] = rhs[a, x] - one * field[1, a, x] - two * field[2, a, x]
    sent_sums(1)


def body(
    right_side,
    diag_blocks,
    off_blocks,
    cell_inverse,
    send_cells,
    recv_index,
    seg_count,
    span_inverse,
    span_couple,
):
    n_gx, n_gy = lax.axis_size("gx"), lax.axis_size("gy")
    vmem = pl.BlockSpec(memory_space=pltpu.VMEM)
    anywhere = pl.BlockSpec(memory_space=pl.ANY)
    smem = pl.BlockSpec(memory_space=pltpu.SMEM)
    shape = jax.ShapeDtypeStruct(right_side.shape, F32)
    dma = pltpu.SemaphoreType.DMA
    scratch = [
        pltpu.VMEM((6, 9, CX, CY, CZ), F32),
        pltpu.VMEM((9, CX, CY, CZ), F32),
        pltpu.VMEM((3, NCHUNK * WIDTH, 128), F32),
        pltpu.VMEM((3, 3, CX, CY, CZ), F32),
        pltpu.VMEM((3, 2, CX, CY, 128), F32),
        pltpu.VMEM((2, CX + 2, 3, CY, CZ), F32),
        pltpu.VMEM((2, 2, CX, 3, CZ), F32),
        pltpu.VMEM((2, 2, CX, 3, CZ), F32),
        pltpu.VMEM((2, 9, 3, ROWS, 128), F32),
        pltpu.VMEM((2, 9, 3, ROWS, 128), F32),
        pltpu.VMEM((2, 9, 3, ROWS, 128), F32),
        pltpu.VMEM((3, ROWS, 128), F32),
        pltpu.VMEM((ROWS, 128), I32),
        pltpu.VMEM((WELLS, 512), I32),
        pltpu.VMEM((WELLS, 512), I32),
        pltpu.VMEM((10, 24, 128), I32),
        pltpu.VMEM((10, 24, 128), I32),
        pltpu.VMEM((CX, CY, CZ), I32),
        pltpu.VMEM((CX, CY, CZ), I32),
        pltpu.VMEM((512, 128), F32),
        pltpu.VMEM((3, 32, 128), F32),
        pltpu.VMEM((3, 32, 128), F32),
        pltpu.VMEM((9, NCHUNK, 128), F32),
        pltpu.VMEM((3, 32, 128), F32),
        pltpu.VMEM((3, NCHUNK, 128), F32),
        pltpu.VMEM((128, 128), F32),
        pltpu.VMEM((2, 2 * n_gy, 1, 128), F32),
        pltpu.VMEM((2, n_gx // 2, 1, 128), F32),
        pltpu.VMEM((8, 128), F32),
        dma((5,)),
        dma((2, 9)),
        dma((2, 9)),
        dma((2, 9)),
        dma((2, 9)),
        dma((2, 4)),
        dma((2, 4)),
        dma((2, 2 * n_gy)),
        dma((2, 2 * n_gy)),
        dma((2, n_gx // 2)),
        dma((2, n_gx // 2)),
    ]
    return pl.pallas_call(
        functools.partial(kernel, n_gx, n_gy),
        out_shape=(shape, shape),
        in_specs=[vmem, vmem, anywhere, anywhere, vmem, vmem, smem, anywhere, vmem],
        out_specs=(vmem, vmem),
        scratch_shapes=scratch,
        compiler_params=pltpu.CompilerParams(collective_id=0, has_side_effects=True),
        name="gmres",
    )(
        right_side,
        diag_blocks,
        off_blocks,
        cell_inverse,
        send_cells,
        recv_index,
        seg_count,
        span_inverse.reshape(NCHUNK * WIDTH, LANES),
        span_couple.transpose(1, 2, 0),
    )


def solution(mesh):
    return jax.shard_map(
        body,
        mesh=mesh,
        in_specs=(
            P(None, "gx", "gy", None),
            P(None, "gx", "gy", None),
            P(None, None, "gx", "gy", None),
            P(None, "gx", "gy", None),
            P(("gx", "gy"), None),
            P(("gx", "gy"), None),
            P(("gx", "gy")),
            P(None, None, ("gx", "gy")),
            P(None, None, ("gx", "gy")),
        ),
        out_specs=(P(None, "gx", "gy", None), P(None, "gx", "gy", None)),
        check_vma=False,
    )
```

```python
import functools

import jax
import jax.numpy as jnp
from jax import lax
from jax.experimental import pallas as pl
from jax.experimental.pallas import tpu as pltpu
from jax.sharding import PartitionSpec as P

CX, CY, CZ = 4, 16, 256
WELLS = 8
MAXSEG = 400
SPAN = 16
NCHUNK = 25
WIDTH = 3 * SPAN
LANES = WELLS * WIDTH
ROWS = 25
MESH = pl.DeviceIdType.MESH
F32, BF16, I32 = jnp.float32, jnp.bfloat16, jnp.int32
NEAR = [(a, b) for a in (-1, 0, 1) for b in (-1, 0, 1)]
ORDER = [7, 1, 3, 5, 6, 8, 0, 2]


def lane_pick(row, lane):
    numbers = lax.GatherDimensionNumbers(
        offset_dims=(),
        collapsed_slice_dims=(1,),
        start_index_map=(1,),
        operand_batching_dims=(0,),
        start_indices_batching_dims=(0,),
    )
    return lax.gather(
        jnp.broadcast_to(row, lane.shape),
        lane[..., None],
        numbers,
        slice_sizes=(1, 1),
        mode=lax.GatherScatterMode.PROMISE_IN_BOUNDS,
    )


def look_up(rows, lane, count, row_at, old=None):
    levels = (count - 1).bit_length()
    bits = [(row_at & (1 << b)) != 0 for b in range(levels)]
    inside = (row_at >= 0) & (row_at < count)

    def tree(a, low, level):
        if level == 0:
            return lane_pick(rows(a, low), lane)
        left = tree(a, low, level - 1)
        if low + (1 << level - 1) >= count:
            return left
        return jnp.where(bits[level - 1], tree(a, low + (1 << level - 1), level - 1), left)

    return [
        jnp.where(inside, tree(a, 0, levels), 0.0 if old is None else old[a]) for a in range(3)
    ]


def kernel(
    n_gx,
    n_gy,
    rhs,
    diag,
    off_hbm,
    cinv_hbm,
    send,
    recv,
    seg_count,
    ginv_hbm,
    couple,
    sol,
    res,
    off,
    cinv,
    ginv,
    field,
    u,
    zp,
    ystage,
    yhalo,
    pool,
    slots,
    back,
    relay,
    ret,
    cell,
    seg_row,
    seg_lane,
    inv_row,
    inv_lane,
    cell_row,
    cell_lane,
    spread,
    y0,
    yp,
    chain,
    ends,
    ytab,
    cpad,
    ar1,
    ar2,
    sums,
    load_sem,
    fwd_send,
    fwd_recv,
    back_send,
    back_recv,
    relay_recv,
    halo_send,
    halo_recv,
    ar1_send,
    ar1_recv,
    ar2_send,
    ar2_recv,
):
    ix = lax.axis_index("gx")
    iy = lax.axis_index("gy")
    core = lax.rem(ix, 2)
    chip = lax.div(ix, 2)
    chips = n_gx // 2
    near = 2 * n_gy

    loads = [
        pltpu.make_async_copy(cinv_hbm, cinv, load_sem.at[0]),
        pltpu.make_async_copy(off_hbm, off, load_sem.at[1]),
    ] + [
        pltpu.make_async_copy(
            ginv_hbm.at[:, j * 128 : j * 128 + 128], ginv.at[j], load_sem.at[2 + j]
        )
        for j in range(3)
    ]
    for load in loads:
        load.start()

    def exists(q):
        a, b = NEAR[q]
        good = True
        if a < 0:
            good = ix > 0
        elif a > 0:
            good = ix < n_gx - 1
        if b < 0:
            good = good & (iy > 0)
        elif b > 0:
            good = good & (iy < n_gy - 1)
        return good

    def device(q):
        if isinstance(q, int):
            return (ix + NEAR[q][0], iy + NEAR[q][1])
        return (ix + lax.div(q, 3) - 1, iy + lax.rem(q, 3) - 1)

    def exists_at(q):
        gx, gy = device(q)
        return (gx >= 0) & (gx < n_gx) & (gy >= 0) & (gy < n_gy) & (q != 4)

    partner = 1 - 2 * core

    def direct(q):
        a, b = NEAR[q]
        return exists(q) & (partner != a) if a and b else exists(q)

    def pair(kind):
        middle = 4 + 3 * partner * jnp.where(kind == 3, 1, jnp.where(kind == 2, -1, 0))
        reach = jnp.where(kind == 1, 3, 1)
        return (middle - reach, middle + reach)

    def near_device(d):
        place = lax.rem(core * n_gy + iy + d, near)
        return (chip * 2 + lax.div(place, n_gy), lax.rem(place, n_gy))

    def far_device(d):
        return (lax.rem(chip + d, chips) * 2 + core, iy)

    barrier = pltpu.get_barrier_semaphore()
    for q in ORDER:

        @pl.when(exists(q))
        def _(q=q):
            pl.semaphore_signal(barrier, inc=1, device_id=device(q), device_id_type=MESH)

    for d in range(1, near):
        pl.semaphore_signal(barrier, inc=1, device_id=near_device(d), device_id_type=MESH)
    for d in range(1, chips):
        pl.semaphore_signal(barrier, inc=1, device_id=far_device(d), device_id_type=MESH)

    def present(edge):
        return jnp.where(edge, 1, 0)

    across_x = 1 + present(ix > 0) + present(ix < n_gx - 1)
    across_y = 1 + present(iy > 0) + present(iy < n_gy - 1)
    greeted = across_x * across_y - 1 + (near - 1) + (chips - 1)

    def fwd_copy(it, q):
        return pltpu.make_async_remote_copy(
            src_ref=pool.at[it, 4],
            dst_ref=pool.at[it, 8 - q],
            send_sem=fwd_send.at[it, q],
            recv_sem=fwd_recv.at[it, 8 - q],
            device_id=device(q),
            device_id_type=MESH,
        )

    def fwd_arrival(it, q):
        return pltpu.make_async_remote_copy(
            src_ref=pool.at[it, 4],
            dst_ref=pool.at[it, q],
            send_sem=fwd_send.at[it, 8 - q],
            recv_sem=fwd_recv.at[it, q],
            device_id=device(q),
            device_id_type=MESH,
        )

    def fwd_relay(it, side):
        b = 2 * side - 1
        return pltpu.make_async_remote_copy(
            src_ref=pool.at[it, 4 + b],
            dst_ref=pool.at[it, 4 - 3 * partner + b],
            send_sem=fwd_send.at[it, 4 + 3 * partner + b],
            recv_sem=fwd_recv.at[it, 4 - 3 * partner + b],
            device_id=(ix + partner, iy),
            device_id_type=MESH,
        )

    def back_relay(it, side):
        q = 4 + 3 * partner + 2 * side - 1
        return pltpu.make_async_remote_copy(
            src_ref=slots.at[it, q],
            dst_ref=relay.at[it, side],
            send_sem=back_send.at[it, q],
            recv_sem=relay_recv.at[it, side],
            device_id=(ix + partner, iy),
            device_id_type=MESH,
        )

    def back_copy(it, q):
        return pltpu.make_async_remote_copy(
            src_ref=slots.at[it, q],
            dst_ref=back.at[it, 8 - q],
            send_sem=back_send.at[it, q],
            recv_sem=back_recv.at[it, 8 - q],
            device_id=device(q),
            device_id_type=MESH,
        )

    side_place = [1, 7, 3, 5]

    def halo_copy(it, side):
        if side < 2:
            src = zp.at[it, 1 if side == 0 else CX]
            dst = zp.at[it, CX + 1 if side == 0 else 0]
        else:
            src = ystage.at[it, side - 2]
            dst = yhalo.at[it, 3 - side]
        other = side ^ 1
        return pltpu.make_async_remote_copy(
            src_ref=src,
            dst_ref=dst,
            send_sem=halo_send.at[it, side],
            recv_sem=halo_recv.at[it, other],
            device_id=device(side_place[side]),
            device_id_type=MESH,
        )

    def near_copy(i, d):
        return pltpu.make_async_remote_copy(
            src_ref=ar1.at[i, 0],
            dst_ref=ar1.at[i, d],
            send_sem=ar1_send.at[i, d],
            recv_sem=ar1_recv.at[i, d],
            device_id=near_device(d),
            device_id_type=MESH,
        )

    def far_copy(i, d):
        return pltpu.make_async_remote_copy(
            src_ref=ar2.at[i, 0],
            dst_ref=ar2.at[i, d],
            send_sem=ar2_send.at[i, d],
            recv_sem=ar2_recv.at[i, d],
            device_id=far_device(d),
            device_id_type=MESH,
        )

    def sent(it, copy, count, place=lambda k: k):
        for k in range(count):
            if place(k) != 4:

                @pl.when(exists(place(k)))
                def _(k=k):
                    copy(it, k).wait_send()

    def sent_halo(it):
        sent(it, halo_copy, 4, lambda side: side_place[side])

    def sent_sums(i):
        for d in range(1, near):
            near_copy(i, d).wait_send()
        for d in range(1, chips):
            far_copy(i, d).wait_send()

    def send_near(i):
        for d in range(1, near):
            near_copy(i, d).start()

    def pass_on(i):
        total = ar1[i, 0]
        for d in range(1, near):
            near_copy(i, d).wait_recv()
            total = total + ar1[i, d]
        ar2[i, 0] = total
        for d in range(1, chips):
            far_copy(i, d).start()

    def collect(i):
        total = ar2[i, 0]
        for d in range(1, chips):
            far_copy(i, d).wait_recv()
            total = total + ar2[i, d]
        return total

    for c in range(ROWS):
        cell[c : c + 1, :] = send[:, c * 128 : (c + 1) * 128]

    field[0] = rhs[...]

    def forward(it):
        for a in range(3):
            total = diag[3 * a] * field[it, 0]
            total = total + diag[3 * a + 1] * field[it, 1]
            total = total + diag[3 * a + 2] * field[it, 2]
            u[a, 0] = total[:, :, :128]
            u[a, 1] = total[:, :, 128:]
        where = cell[...]
        high = where >> 7
        lane = where & 127
        sub = lax.broadcasted_iota(I32, (8, 128), 0)
        tiles = [slice(8 * i, 8 * i + 8) for i in range(3)]
        end_high = jnp.broadcast_to(high[24:25], (8, 128)) - 2 * sub
        end_lane = jnp.broadcast_to(lane[24:25], (8, 128))

        def step(g, got):
            got = list(got)
            for i, tile in enumerate(tiles):
                base = high[tile] - 64 * g
                new = look_up(
                    lambda a, r: u[a, r % 2, 2 * g + r // 32, r // 2 % 16 : r // 2 % 16 + 1, :],
                    lane[tile],
                    64,
                    base,
                    got[3 * i : 3 * i + 3],
                )
                got[3 * i : 3 * i + 3] = new
            base = end_high - 64 * g
            for r in range(0, 32, 8):
                for half in range(2):
                    match = base == 2 * r + half
                    for a in range(3):
                        here = u[a, half, 2 * g + r // 16, r % 16 : r % 16 + 8, :]
                        value = lane_pick(here, end_lane)
                        got[9 + a] = jnp.where(match, value, got[9 + a])
            return tuple(got)

        none = jnp.zeros((8, 128), F32)
        got = lax.fori_loop(0, CX // 2, step, tuple([none] * 12))
        for a in range(3):
            for i, tile in enumerate(tiles):
                pool[it, 4, a, tile] = got[3 * i + a]
            pool[it, 4, a, 24:25] = jnp.sum(got[9 + a], axis=0, keepdims=True)

    def send_forward(it):
        for q in ORDER:

            @pl.when(direct(q))
            def _(q=q):
                fwd_copy(it, q).start()

    def setup():
        total = jnp.zeros((CX * CY, 2 * CZ), F32)
        for start, width in ((0, 1024), (1024, 1024), (2048, 1024), (3072, 128)):
            where = send[:, start : start + width]
            slot = lax.broadcasted_iota(I32, (1, width), 1) + start
            left = lax.broadcasted_iota(I32, (CX * CY, width), 0) == (where >> 8)
            hit = lax.broadcasted_iota(I32, (CZ, width), 0) == (where & 255)
            row = jnp.where(hit, ((slot >> 7) + 1).astype(F32), 0.0)
            lane = jnp.where(hit, (slot & 127).astype(F32), 0.0)
            total = total + lax.dot_general(
                jnp.where(left, 1.0, 0.0).astype(BF16),
                jnp.concatenate([row, lane], axis=0).astype(BF16),
                (((1,), (1,)), ((), ())),
                preferred_element_type=F32,
            )
        cell_row[...] = total[:, :CZ].astype(I32).reshape(CX, CY, CZ) - 1
        cell_lane[...] = total[:, CZ:].astype(I32).reshape(CX, CY, CZ)

        seg_lane[...] = jnp.zeros(seg_lane.shape, I32)
        seg_lane[:, :MAXSEG] = recv[...]
        position = seg_lane[...]
        well = lax.broadcasted_iota(I32, (WELLS, 512), 0)
        segment = lax.broadcasted_iota(I32, (WELLS, 512), 1)
        count = jnp.zeros((WELLS, 512), I32)
        for w in range(WELLS):
            count = jnp.where(well == w, seg_count[w], count)
        live = (segment < count) & (segment < MAXSEG)
        high = position >> 7
        seg_row[...] = jnp.where(live, high, -1)
        seg_lane[...] = position & 127

        sub232 = lax.broadcasted_iota(I32, (232, 512), 0)
        sub128 = lax.broadcasted_iota(I32, (128, 512), 0)
        along = lax.broadcasted_iota(I32, (1, 512), 1)
        total = jnp.zeros((232, 256), F32)
        for w in range(WELLS):
            high = seg_row[w : w + 1, :]
            slab = (high * 1311) >> 15
            row_in = high - ROWS * slab
            goal = jnp.where(row_in == ROWS - 1, 9 * 24 + slab, 24 * slab + row_in)
            left = sub232 == jnp.where(high < 0, -1, goal)
            hit = sub128 == seg_lane[w : w + 1, :]
            row = jnp.where(hit, ((along >> 4) + 1).astype(F32), 0.0)
            lane = jnp.where(hit, ((along & 15) + w * SPAN).astype(F32), 0.0)
            total = total + lax.dot_general(
                jnp.where(left, 1.0, 0.0).astype(BF16),
                jnp.concatenate([row, lane], axis=0).astype(BF16),
                (((1,), (1,)), ((), ())),
                preferred_element_type=F32,
            )
        for q in range(9):
            inv_row[q] = total[24 * q : 24 * q + 24, :128].astype(I32) - 1
            inv_lane[q] = total[24 * q : 24 * q + 24, 128:].astype(I32)
        inv_row[9, 0:16] = total[216:232, :128].astype(I32) - 1
        inv_lane[9, 0:16] = total[216:232, 128:].astype(I32)

        for j in range(3):
            loads[2 + j].wait()
        y0[...] = jnp.zeros(y0.shape, F32)
        group = lax.broadcasted_iota(I32, (32, 128), 1) >> 4
        firsts = []
        for k in range(3):
            for j in range(3):
                y0[j, 0:NCHUNK] = ginv[j, pl.ds(k, NCHUNK, stride=WIDTH), :]
            firsts.append(permuted())
        pairs = []
        cpad[...] = jnp.zeros(cpad.shape, F32)
        for kb in range(9):
            cpad[0:WELLS, 0:NCHUNK] = couple[kb]
            pairs.append(lane_pick(cpad[...].T[0:32], group)[:NCHUNK])
        for a in range(3):
            for b in range(3):
                total = firsts[0][a][:NCHUNK] * pairs[b]
                for k in (1, 2):
                    total = total + firsts[k][a][:NCHUNK] * pairs[3 * k + b]
                chain[3 * a + b] = total
        for b in range(3):
            ends[b, 0:8] = jnp.zeros((8, 128), F32)

    def permuted():
        lane = lax.broadcasted_iota(I32, (8, 128), 1)
        result = []
        for a in range(3):
            source = (lane >> 4) * WIDTH + 3 * (lane & 15) + a
            tiles = [None] * 4
            for j in range(3):
                here = (source >> 7) == j
                for i in range(4):
                    value = lane_pick(y0[j, 8 * i : 8 * i + 8], source & 127)
                    tiles[i] = value if j == 0 else jnp.where(here, value, tiles[i])
            result.append(jnp.concatenate(tiles, axis=0))
        return result

    def wells(it):
        row_of = seg_row[...]
        lane_of = seg_lane[...]
        tiles = [slice(128 * i, 128 * i + 128) for i in range(3)]
        sub = lax.broadcasted_iota(I32, (8, 128), 0)
        along = lax.broadcasted_iota(I32, (8, 128), 1)
        mine = (along >> 4) == sub

        def one_row(values):
            value = lane_pick(values[:, 384:], along & 15)
            return jnp.sum(jnp.where(mine, value, 0), axis=0, keepdims=True)

        end_row = jnp.broadcast_to(one_row(row_of), (8, 128)) - sub
        end_lane = jnp.broadcast_to(one_row(lane_of), (8, 128))

        def take(q, got):
            got = list(got)
            for i, tile in enumerate(tiles):
                base = row_of[:, tile] - q * ROWS
                new = look_up(
                    lambda a, r: pool[it, q, a, r : r + 1, :],
                    lane_of[:, tile],
                    ROWS,
                    base,
                    got[3 * i : 3 * i + 3],
                )
                got[3 * i : 3 * i + 3] = new
            base = end_row - q * ROWS
            for r in range(0, 24, 8):
                match = base == r
                for a in range(3):
                    value = lane_pick(pool[it, q, a, r : r + 8, :], end_lane)
                    got[9 + a] = jnp.where(match, value, got[9 + a])
            match = (base == 24) & (sub == 0)
            for a in range(3):
                value = lane_pick(pool[it, q, a, 24:25, :], end_lane)
                got[9 + a] = jnp.where(match, value, got[9 + a])
            return tuple(got)

        def step(p, got):
            low, high = pair(p)
            for side in (low, high):

                @pl.when(exists_at(side) & (p > 0))
                def _(side=side):
                    fwd_arrival(it, side).wait_recv()

            return take(high, take(low, got))

        none = jnp.zeros((WELLS, 128), F32)
        got = take(4, tuple([none] * 12))
        for side in range(2):

            @pl.when(exists(3 + 2 * side))
            def _(side=side):
                fwd_arrival(it, 3 + 2 * side).wait_recv()
                fwd_relay(it, side).start()

        got = list(lax.fori_loop(0, 4, step, got))
        for a in range(3):
            value = jnp.sum(got[9 + a], axis=0, keepdims=True)
            value = lane_pick(value, (sub * 16 + along) & 127)
            got[9 + a] = jnp.where(along < 16, value, 0.0)
        none = jnp.zeros((WELLS, 128), F32)
        for i in range(4):
            square = jnp.concatenate([got[3 * i + a] for a in range(3)] + [none] * 13, axis=0)
            spread[128 * i : 128 * i + 128] = square.T
        well = [(along + 128 * j) // WIDTH for j in range(3)]
        for j in range(3):
            totals = [None] * NCHUNK
            for a in range(3):
                for c in range(NCHUNK):
                    for at in (SPAN * c, SPAN * c + 8):
                        r = lane_pick(spread[at : at + 8], well[j] + 8 * a)
                        g = ginv[j, pl.ds(3 * at + a, 8, stride=3), :]
                        totals[c] = g * r if totals[c] is None else totals[c] + g * r
            for c in range(NCHUNK):
                y0[j, c : c + 1, :] = jnp.sum(totals[c], axis=0, keepdims=True)
        moved = permuted()
        for a in range(3):
            yp[a] = moved[a]

        def link(c, last):
            new = []
            for a in range(3):
                value = yp[a, pl.ds(c, 1), :]
                for b in range(3):
                    value = value - chain[3 * a + b, pl.ds(c, 1), :] * last[b]
                new.append(value)
            for a in range(3):
                ends[a, pl.ds(c + 1, 1), :] = new[a]
            return tuple(new)

        lax.fori_loop(0, NCHUNK, link, tuple([jnp.zeros((1, 128), F32)] * 3), unroll=5)
        last_lane = lax.broadcasted_iota(I32, (NCHUNK, 128), 1) | 15
        before = [lane_pick(ends[b, 0:NCHUNK, :], last_lane) for b in range(3)]
        for a in range(3):
            value = yp[a, 0:NCHUNK]
            for b in range(3):
                value = value - chain[3 * a + b] * before[b]
            ytab[a] = value

        def corrections(row_at, lane_at):
            return look_up(lambda a, r: ytab[a, r : r + 1, :], lane_at, ROWS, row_at)

        for half in range(2):
            tile = slice(8 * half, 8 * half + 8)
            got = corrections(inv_row[9, tile], inv_lane[9, tile])
            for q in range(8 * half, min(9, 8 * half + 8)):
                for a in range(3):
                    slots[it, q, a, 24:25] = got[a][q - 8 * half : q - 8 * half + 1]

        def give(q):
            for i in range(3):
                tile = slice(8 * i, 8 * i + 8)
                got = corrections(inv_row[q, tile], inv_lane[q, tile])
                for a in range(3):
                    slots[it, q, a, tile] = got[a]

        def give_pair(t, carry):
            kind = jnp.where(t == 2, 0, jnp.where(t == 3, 1, 3 - t))
            for side, q in enumerate(pair(kind)):
                give(q)

            for side, q in enumerate(pair(kind)):

                @pl.when(exists_at(q) & (t == 0))
                def _(side=side):
                    back_relay(it, side).start()

                @pl.when(exists_at(q) & (t == 2))
                def _(side=side):
                    back_relay(it, side).wait_recv()
                    here = slots[it, 3 + 2 * side] + relay[it, side]
                    slots[it, 3 + 2 * side] = here

                @pl.when(exists_at(q) & (t > 0))
                def _(q=q):
                    back_copy(it, q).start()

            return carry

        lax.fori_loop(0, 4, give_pair, 0)
        give(4)

    def backward(it):
        ret[...] = slots[it, 4]
        for q in ORDER:

            @pl.when(direct(q))
            def _(q=q):
                back_copy(it, 8 - q).wait_recv()
                ret[...] = ret[...] + back[it, q]

        def plane(x):
            for i in range(2):
                sides = []
                for half in range(2):
                    tile = (slice(8 * i, 8 * i + 8), slice(128 * half, 128 * half + 128))
                    row_at = cell_row[(x,) + tile]
                    lane_at = cell_lane[(x,) + tile]
                    got = look_up(lambda a, r: ret[a, r : r + 1, :], lane_at, ROWS, row_at)
                    for a in range(3):
                        value = got[a]
                        for b in range(3):
                            value = value + cinv[(3 * a + b, x) + tile] * field[(it, b, x) + tile]
                        zp[(it, x + 1, a) + tile] = value
                        if i == 0:
                            ystage[it, 0, x, a : a + 1, tile[1]] = value[0:1]
                        else:
                            ystage[it, 1, x, a : a + 1, tile[1]] = value[7:8]

        def planes(t, carry):
            plane(t)
            plane(3 - t)

            @pl.when((t == 0) & exists(1))
            def _():
                halo_copy(it, 0).start()

            @pl.when((t == 0) & exists(7))
            def _():
                halo_copy(it, 1).start()

            return carry

        lax.fori_loop(0, 2, planes, 0)
        start_halo(it, 2)
        start_halo(it, 3)

    def start_halo(it, side):
        @pl.when(exists(side_place[side]))
        def _():
            halo_copy(it, side).start()

    def jacobian(it, between=lambda: None):
        row = lax.broadcasted_iota(I32, (CY, CZ), 0)
        column = lax.broadcasted_iota(I32, (CY, CZ), 1)
        for x in range(CX):
            total = [None] * 3

            def add(blocks, value, b):
                for a in range(3):
                    term = blocks(3 * a + b) * value
                    total[a] = term if total[a] is None else total[a] + term

            for b in range(3):
                here = zp[it, x + 1, b]
                add(lambda e: diag[e, x], here, b)
                if x > 0:
                    add(lambda e: off[0, e, x], zp[it, x, b], b)
                if x < CX - 1:
                    add(lambda e: off[1, e, x], zp[it, x + 2, b], b)
                value = jnp.where(row > 0, pltpu.roll(here, 1, 0), 0.0)
                add(lambda e: off[2, e, x], value, b)
                value = jnp.where(row < CY - 1, pltpu.roll(here, CY - 1, 0), 0.0)
                add(lambda e: off[3, e, x], value, b)
                value = jnp.where(column > 0, pltpu.roll(here, 1, 1), 0.0)
                add(lambda e: off[4, e, x], value, b)
                value = jnp.where(column < CZ - 1, pltpu.roll(here, CZ - 1, 1), 0.0)
                add(lambda e: off[5, e, x], value, b)
            for a in range(3):
                field[it + 1, a, x] = total[a]

        result = between()
        for side in range(4):

            @pl.when(exists(side_place[side]))
            def _(side=side):
                halo_copy(it, side ^ 1).wait_recv()
                if side < 2:
                    x = 0 if side == 0 else CX - 1
                    plane = 0 if side == 0 else CX + 1
                    for a in range(3):
                        value = field[it + 1, a, x]
                        for b in range(3):
                            value = value + off[side, 3 * a + b, x] * zp[it, plane, b]
                        field[it + 1, a, x] = value
                else:
                    y = 0 if side == 2 else CY - 1
                    for x in range(CX):
                        for a in range(3):
                            value = field[it + 1, a, x, y : y + 1, :]
                            for b in range(3):
                                beside = yhalo[it, side - 2, x, b : b + 1, :]
                                value = value + off[side, 3 * a + b, x, y : y + 1, :] * beside
                            field[it + 1, a, x, y : y + 1, :] = value
        return result

    def dot_row(place, first, second):
        total = None
        for a in range(3):
            for x in range(CX):
                product = first(a, x) * second(a, x)
                total = product if total is None else total + product
        total = jnp.sum(total, axis=0, keepdims=True)
        sums[place : place + 1, :] = total[:, :128] + total[:, 128:]

    def pack_sums(i):
        sub = lax.broadcasted_iota(I32, (8, 128), 0)
        along = lax.broadcasted_iota(I32, (8, 128), 1)
        total = jnp.sum(sums[...], axis=1, keepdims=True)
        ar1[i, 0] = jnp.sum(jnp.where(sub == along, total, 0.0), axis=0, keepdims=True)

    sums[...] = jnp.zeros((8, 128), F32)

    r_of = lambda a, x: rhs[a, x]
    w1_of = lambda a, x: field[1, a, x]
    w2_of = lambda a, x: field[2, a, x]
    v2_of = lambda a, x: field[0, a, x]

    forward(0)
    pl.semaphore_wait(barrier, greeted)
    send_forward(0)
    setup()
    wells(0)
    sent(0, fwd_copy, 9)
    loads[0].wait()
    backward(0)
    loads[1].wait()
    jacobian(0)
    forward(1)
    send_forward(1)
    dot_row(0, r_of, r_of)
    dot_row(1, w1_of, r_of)
    pack_sums(0)
    send_near(0)
    sent(0, back_copy, 9)
    sent_halo(0)
    wells(1)
    pass_on(0)
    sent(1, fwd_copy, 9)
    backward(1)

    def between():
        first = collect(0)
        square = first[:, 0:1]
        along = first[:, 1:2] / square
        for a in range(3):
            for x in range(CX):
                field[0, a, x] = field[1, a, x] - along * rhs[a, x]
        dot_row(0, v2_of, v2_of)
        dot_row(4, v2_of, r_of)
        return square, along

    square, along = jacobian(1, between)
    for a in range(3):
        for x in range(CX):
            field[2, a, x] = field[2, a, x] - along * field[1, a, x]
    dot_row(1, w2_of, r_of)
    dot_row(2, w2_of, v2_of)
    dot_row(3, w2_of, w2_of)
    pack_sums(1)
    send_near(1)
    sent(1, back_copy, 9)
    sent_halo(1)
    sent_sums(0)
    pass_on(1)
    second = collect(1)

    beta = jnp.sqrt(square)
    size = jnp.sqrt(second[:, 0:1])
    top_first = along
    sub_first = size / beta
    top_second = second[:, 1:2] / (size * beta)
    mid_second = second[:, 2:3] / (size * size) - top_second * (second[:, 4:5] / (size * beta))
    gram_first = top_first * top_first + sub_first * sub_first
    gram_cross = top_first * top_second + sub_first * mid_second
    gram_second = second[:, 3:4] / (size * size)
    determinant = gram_first * gram_second - gram_cross * gram_cross
    weight_one = (gram_second * beta * top_first - gram_cross * beta * top_second) / determinant
    weight_two = (gram_first * beta * top_second - gram_cross * beta * top_first) / determinant
    one = weight_one / beta
    two = weight_two / size
    mixed = one - two * along
    for a in range(3):
        for x in range(CX):
            sol[a, x] = mixed * zp[0, x + 1, a] + two * zp[1, x + 1, a]
            res[a, x] = rhs[a, x] - one * field[1, a, x] - two * field[2, a, x]
    sent_sums(1)


def body(
    right_side,
    diag_blocks,
    off_blocks,
    cell_inverse,
    send_cells,
    recv_index,
    seg_count,
    span_inverse,
    span_couple,
):
    n_gx, n_gy = lax.axis_size("gx"), lax.axis_size("gy")
    vmem = pl.BlockSpec(memory_space=pltpu.VMEM)
    anywhere = pl.BlockSpec(memory_space=pl.ANY)
    smem = pl.BlockSpec(memory_space=pltpu.SMEM)
    shape = jax.ShapeDtypeStruct(right_side.shape, F32)
    dma = pltpu.SemaphoreType.DMA
    scratch = [
        pltpu.VMEM((6, 9, CX, CY, CZ), F32),
        pltpu.VMEM((9, CX, CY, CZ), F32),
        pltpu.VMEM((3, NCHUNK * WIDTH, 128), F32),
        pltpu.VMEM((3, 3, CX, CY, CZ), F32),
        pltpu.VMEM((3, 2, CX, CY, 128), F32),
        pltpu.VMEM((2, CX + 2, 3, CY, CZ), F32),
        pltpu.VMEM((2, 2, CX, 3, CZ), F32),
        pltpu.VMEM((2, 2, CX, 3, CZ), F32),
        pltpu.VMEM((2, 9, 3, ROWS, 128), F32),
        pltpu.VMEM((2, 9, 3, ROWS, 128), F32),
        pltpu.VMEM((2, 9, 3, ROWS, 128), F32),
        pltpu.VMEM((2, 2, 3, ROWS, 128), F32),
        pltpu.VMEM((3, ROWS, 128), F32),
        pltpu.VMEM((ROWS, 128), I32),
        pltpu.VMEM((WELLS, 512), I32),
        pltpu.VMEM((WELLS, 512), I32),
        pltpu.VMEM((10, 24, 128), I32),
        pltpu.VMEM((10, 24, 128), I32),
        pltpu.VMEM((CX, CY, CZ), I32),
        pltpu.VMEM((CX, CY, CZ), I32),
        pltpu.VMEM((512, 128), F32),
        pltpu.VMEM((3, 32, 128), F32),
        pltpu.VMEM((3, 32, 128), F32),
        pltpu.VMEM((9, NCHUNK, 128), F32),
        pltpu.VMEM((3, 32, 128), F32),
        pltpu.VMEM((3, NCHUNK, 128), F32),
        pltpu.VMEM((128, 128), F32),
        pltpu.VMEM((2, 2 * n_gy, 1, 128), F32),
        pltpu.VMEM((2, n_gx // 2, 1, 128), F32),
        pltpu.VMEM((8, 128), F32),
        dma((5,)),
        dma((2, 9)),
        dma((2, 9)),
        dma((2, 9)),
        dma((2, 9)),
        dma((2, 2)),
        dma((2, 4)),
        dma((2, 4)),
        dma((2, 2 * n_gy)),
        dma((2, 2 * n_gy)),
        dma((2, n_gx // 2)),
        dma((2, n_gx // 2)),
    ]
    return pl.pallas_call(
        functools.partial(kernel, n_gx, n_gy),
        out_shape=(shape, shape),
        in_specs=[vmem, vmem, anywhere, anywhere, vmem, vmem, smem, anywhere, vmem],
        out_specs=(vmem, vmem),
        scratch_shapes=scratch,
        compiler_params=pltpu.CompilerParams(collective_id=0, has_side_effects=True),
        name="gmres",
    )(
        right_side,
        diag_blocks,
        off_blocks,
        cell_inverse,
        send_cells,
        recv_index,
        seg_count,
        span_inverse.reshape(NCHUNK * WIDTH, LANES),
        span_couple.transpose(1, 2, 0),
    )


def solution(mesh):
    return jax.shard_map(
        body,
        mesh=mesh,
        in_specs=(
            P(None, "gx", "gy", None),
            P(None, "gx", "gy", None),
            P(None, None, "gx", "gy", None),
            P(None, "gx", "gy", None),
            P(("gx", "gy"), None),
            P(("gx", "gy"), None),
            P(("gx", "gy")),
            P(None, None, ("gx", "gy")),
            P(None, None, ("gx", "gy")),
        ),
        out_specs=(P(None, "gx", "gy", None), P(None, "gx", "gy", None)),
        check_vma=False,
    )
```

```python
import functools

import jax
import jax.numpy as jnp
from jax import lax
from jax.experimental import pallas as pl
from jax.experimental.pallas import tpu as pltpu
from jax.sharding import PartitionSpec as P

CX, CY, CZ = 4, 16, 256
WELLS = 8
MAXSEG = 400
SPAN = 16
NCHUNK = 25
WIDTH = 3 * SPAN
LANES = WELLS * WIDTH
ROWS = 25
MESH = pl.DeviceIdType.MESH
F32, BF16, I32 = jnp.float32, jnp.bfloat16, jnp.int32
NEAR = [(a, b) for a in (-1, 0, 1) for b in (-1, 0, 1)]
ORDER = [7, 1, 3, 5, 6, 8, 0, 2]


def lane_pick(row, lane):
    numbers = lax.GatherDimensionNumbers(
        offset_dims=(),
        collapsed_slice_dims=(1,),
        start_index_map=(1,),
        operand_batching_dims=(0,),
        start_indices_batching_dims=(0,),
    )
    return lax.gather(
        jnp.broadcast_to(row, lane.shape),
        lane[..., None],
        numbers,
        slice_sizes=(1, 1),
        mode=lax.GatherScatterMode.PROMISE_IN_BOUNDS,
    )


def look_up(rows, lane, count, row_at, old=None):
    levels = (count - 1).bit_length()
    bits = [(row_at & (1 << b)) != 0 for b in range(levels)]
    inside = (row_at >= 0) & (row_at < count)

    def tree(a, low, level):
        if level == 0:
            return lane_pick(rows(a, low), lane)
        left = tree(a, low, level - 1)
        if low + (1 << level - 1) >= count:
            return left
        return jnp.where(bits[level - 1], tree(a, low + (1 << level - 1), level - 1), left)

    return [
        jnp.where(inside, tree(a, 0, levels), 0.0 if old is None else old[a]) for a in range(3)
    ]


def kernel(
    n_gx,
    n_gy,
    rhs,
    diag,
    off_hbm,
    cinv_hbm,
    send,
    recv,
    seg_count,
    ginv_hbm,
    couple,
    z_out,
    w_out,
    weights,
    off,
    cinv,
    ginv,
    field,
    u,
    zp,
    ystage,
    yhalo,
    pool,
    slots,
    back,
    relay,
    ret,
    cell,
    seg_row,
    seg_lane,
    inv_row,
    inv_lane,
    cell_row,
    cell_lane,
    spread,
    y0,
    yp,
    chain,
    ends,
    ytab,
    cpad,
    ar1,
    ar2,
    sums,
    load_sem,
    fwd_send,
    fwd_recv,
    back_send,
    back_recv,
    relay_recv,
    halo_send,
    halo_recv,
    ar1_send,
    ar1_recv,
    ar2_send,
    ar2_recv,
):
    ix = lax.axis_index("gx")
    iy = lax.axis_index("gy")
    core = lax.rem(ix, 2)
    chip = lax.div(ix, 2)
    chips = n_gx // 2
    near = 2 * n_gy

    loads = [
        pltpu.make_async_copy(cinv_hbm, cinv, load_sem.at[0]),
        pltpu.make_async_copy(off_hbm, off, load_sem.at[1]),
    ] + [
        pltpu.make_async_copy(
            ginv_hbm.at[:, j * 128 : j * 128 + 128], ginv.at[j], load_sem.at[2 + j]
        )
        for j in range(3)
    ]
    for load in loads:
        load.start()

    def exists(q):
        a, b = NEAR[q]
        good = True
        if a < 0:
            good = ix > 0
        elif a > 0:
            good = ix < n_gx - 1
        if b < 0:
            good = good & (iy > 0)
        elif b > 0:
            good = good & (iy < n_gy - 1)
        return good

    def device(q):
        if isinstance(q, int):
            return (ix + NEAR[q][0], iy + NEAR[q][1])
        return (ix + lax.div(q, 3) - 1, iy + lax.rem(q, 3) - 1)

    def exists_at(q):
        gx, gy = device(q)
        return (gx >= 0) & (gx < n_gx) & (gy >= 0) & (gy < n_gy) & (q != 4)

    partner = 1 - 2 * core

    def direct(q):
        a, b = NEAR[q]
        return exists(q) & (partner != a) if a and b else exists(q)

    def pair(kind):
        middle = 4 + 3 * partner * jnp.where(kind == 3, 1, jnp.where(kind == 2, -1, 0))
        reach = jnp.where(kind == 1, 3, 1)
        return (middle - reach, middle + reach)

    def near_device(d):
        place = lax.rem(core * n_gy + iy + d, near)
        return (chip * 2 + lax.div(place, n_gy), lax.rem(place, n_gy))

    def far_device(d):
        return (lax.rem(chip + d, chips) * 2 + core, iy)

    barrier = pltpu.get_barrier_semaphore()
    for q in ORDER:

        @pl.when(exists(q))
        def _(q=q):
            pl.semaphore_signal(barrier, inc=1, device_id=device(q), device_id_type=MESH)

    for d in range(1, near):
        pl.semaphore_signal(barrier, inc=1, device_id=near_device(d), device_id_type=MESH)
    for d in range(1, chips):
        pl.semaphore_signal(barrier, inc=1, device_id=far_device(d), device_id_type=MESH)

    def present(edge):
        return jnp.where(edge, 1, 0)

    across_x = 1 + present(ix > 0) + present(ix < n_gx - 1)
    across_y = 1 + present(iy > 0) + present(iy < n_gy - 1)
    greeted = across_x * across_y - 1 + (near - 1) + (chips - 1)

    def fwd_copy(it, q):
        return pltpu.make_async_remote_copy(
            src_ref=pool.at[it, 4],
            dst_ref=pool.at[it, 8 - q],
            send_sem=fwd_send.at[it, q],
            recv_sem=fwd_recv.at[it, 8 - q],
            device_id=device(q),
            device_id_type=MESH,
        )

    def fwd_arrival(it, q):
        return pltpu.make_async_remote_copy(
            src_ref=pool.at[it, 4],
            dst_ref=pool.at[it, q],
            send_sem=fwd_send.at[it, 8 - q],
            recv_sem=fwd_recv.at[it, q],
            device_id=device(q),
            device_id_type=MESH,
        )

    def fwd_relay(it, side):
        b = 2 * side - 1
        return pltpu.make_async_remote_copy(
            src_ref=pool.at[it, 4 + b],
            dst_ref=pool.at[it, 4 - 3 * partner + b],
            send_sem=fwd_send.at[it, 4 + 3 * partner + b],
            recv_sem=fwd_recv.at[it, 4 - 3 * partner + b],
            device_id=(ix + partner, iy),
            device_id_type=MESH,
        )

    def back_relay(it, side):
        q = 4 + 3 * partner + 2 * side - 1
        return pltpu.make_async_remote_copy(
            src_ref=slots.at[it, q],
            dst_ref=relay.at[it, side],
            send_sem=back_send.at[it, q],
            recv_sem=relay_recv.at[it, side],
            device_id=(ix + partner, iy),
            device_id_type=MESH,
        )

    def back_copy(it, q):
        return pltpu.make_async_remote_copy(
            src_ref=slots.at[it, q],
            dst_ref=back.at[it, 8 - q],
            send_sem=back_send.at[it, q],
            recv_sem=back_recv.at[it, 8 - q],
            device_id=device(q),
            device_id_type=MESH,
        )

    side_place = [1, 7, 3, 5]

    def halo_copy(it, side):
        if side < 2:
            src = zp.at[it, 1 if side == 0 else CX]
            dst = zp.at[it, CX + 1 if side == 0 else 0]
        else:
            src = ystage.at[it, side - 2]
            dst = yhalo.at[it, 3 - side]
        other = side ^ 1
        return pltpu.make_async_remote_copy(
            src_ref=src,
            dst_ref=dst,
            send_sem=halo_send.at[it, side],
            recv_sem=halo_recv.at[it, other],
            device_id=device(side_place[side]),
            device_id_type=MESH,
        )

    def near_copy(i, d):
        return pltpu.make_async_remote_copy(
            src_ref=ar1.at[i, 0],
            dst_ref=ar1.at[i, d],
            send_sem=ar1_send.at[i, d],
            recv_sem=ar1_recv.at[i, d],
            device_id=near_device(d),
            device_id_type=MESH,
        )

    def far_copy(i, d):
        return pltpu.make_async_remote_copy(
            src_ref=ar2.at[i, 0],
            dst_ref=ar2.at[i, d],
            send_sem=ar2_send.at[i, d],
            recv_sem=ar2_recv.at[i, d],
            device_id=far_device(d),
            device_id_type=MESH,
        )

    def sent(it, copy, count, place=lambda k: k):
        for k in range(count):
            if place(k) != 4:

                @pl.when(exists(place(k)))
                def _(k=k):
                    copy(it, k).wait_send()

    def sent_halo(it):
        sent(it, halo_copy, 4, lambda side: side_place[side])

    def sent_sums(i):
        for d in range(1, near):
            near_copy(i, d).wait_send()
        for d in range(1, chips):
            far_copy(i, d).wait_send()

    def send_near(i):
        for d in range(1, near):
            near_copy(i, d).start()

    def pass_on(i):
        total = ar1[i, 0]
        for d in range(1, near):
            near_copy(i, d).wait_recv()
            total = total + ar1[i, d]
        ar2[i, 0] = total
        for d in range(1, chips):
            far_copy(i, d).start()

    def collect(i):
        total = ar2[i, 0]
        for d in range(1, chips):
            far_copy(i, d).wait_recv()
            total = total + ar2[i, d]
        return total

    for c in range(ROWS):
        cell[c : c + 1, :] = send[:, c * 128 : (c + 1) * 128]

    field[0] = rhs[...]

    def forward(it):
        for a in range(3):
            total = diag[3 * a] * field[it, 0]
            total = total + diag[3 * a + 1] * field[it, 1]
            total = total + diag[3 * a + 2] * field[it, 2]
            u[a, 0] = total[:, :, :128]
            u[a, 1] = total[:, :, 128:]
        where = cell[...]
        high = where >> 7
        lane = where & 127
        sub = lax.broadcasted_iota(I32, (8, 128), 0)
        tiles = [slice(8 * i, 8 * i + 8) for i in range(3)]
        end_high = jnp.broadcast_to(high[24:25], (8, 128)) - 2 * sub
        end_lane = jnp.broadcast_to(lane[24:25], (8, 128))

        def step(g, got):
            got = list(got)
            for i, tile in enumerate(tiles):
                base = high[tile] - 64 * g
                new = look_up(
                    lambda a, r: u[a, r % 2, 2 * g + r // 32, r // 2 % 16 : r // 2 % 16 + 1, :],
                    lane[tile],
                    64,
                    base,
                    got[3 * i : 3 * i + 3],
                )
                got[3 * i : 3 * i + 3] = new
            base = end_high - 64 * g
            for r in range(0, 32, 8):
                for half in range(2):
                    match = base == 2 * r + half
                    for a in range(3):
                        here = u[a, half, 2 * g + r // 16, r % 16 : r % 16 + 8, :]
                        value = lane_pick(here, end_lane)
                        got[9 + a] = jnp.where(match, value, got[9 + a])
            return tuple(got)

        none = jnp.zeros((8, 128), F32)
        got = lax.fori_loop(0, CX // 2, step, tuple([none] * 12))
        for a in range(3):
            for i, tile in enumerate(tiles):
                pool[it, 4, a, tile] = got[3 * i + a]
            pool[it, 4, a, 24:25] = jnp.sum(got[9 + a], axis=0, keepdims=True)

    def send_forward(it):
        for q in ORDER:

            @pl.when(direct(q))
            def _(q=q):
                fwd_copy(it, q).start()

    def setup():
        total = jnp.zeros((CX * CY, 2 * CZ), F32)
        for start, width in ((0, 1024), (1024, 1024), (2048, 1024), (3072, 128)):
            where = send[:, start : start + width]
            slot = lax.broadcasted_iota(I32, (1, width), 1) + start
            left = lax.broadcasted_iota(I32, (CX * CY, width), 0) == (where >> 8)
            hit = lax.broadcasted_iota(I32, (CZ, width), 0) == (where & 255)
            row = jnp.where(hit, ((slot >> 7) + 1).astype(F32), 0.0)
            lane = jnp.where(hit, (slot & 127).astype(F32), 0.0)
            total = total + lax.dot_general(
                jnp.where(left, 1.0, 0.0).astype(BF16),
                jnp.concatenate([row, lane], axis=0).astype(BF16),
                (((1,), (1,)), ((), ())),
                preferred_element_type=F32,
            )
        cell_row[...] = total[:, :CZ].astype(I32).reshape(CX, CY, CZ) - 1
        cell_lane[...] = total[:, CZ:].astype(I32).reshape(CX, CY, CZ)

        seg_lane[...] = jnp.zeros(seg_lane.shape, I32)
        seg_lane[:, :MAXSEG] = recv[...]
        position = seg_lane[...]
        well = lax.broadcasted_iota(I32, (WELLS, 512), 0)
        segment = lax.broadcasted_iota(I32, (WELLS, 512), 1)
        count = jnp.zeros((WELLS, 512), I32)
        for w in range(WELLS):
            count = jnp.where(well == w, seg_count[w], count)
        live = (segment < count) & (segment < MAXSEG)
        high = position >> 7
        seg_row[...] = jnp.where(live, high, -1)
        seg_lane[...] = position & 127

        sub232 = lax.broadcasted_iota(I32, (232, 512), 0)
        sub128 = lax.broadcasted_iota(I32, (128, 512), 0)
        along = lax.broadcasted_iota(I32, (1, 512), 1)
        total = jnp.zeros((232, 256), F32)
        for w in range(WELLS):
            high = seg_row[w : w + 1, :]
            slab = (high * 1311) >> 15
            row_in = high - ROWS * slab
            goal = jnp.where(row_in == ROWS - 1, 9 * 24 + slab, 24 * slab + row_in)
            left = sub232 == jnp.where(high < 0, -1, goal)
            hit = sub128 == seg_lane[w : w + 1, :]
            row = jnp.where(hit, ((along >> 4) + 1).astype(F32), 0.0)
            lane = jnp.where(hit, ((along & 15) + w * SPAN).astype(F32), 0.0)
            total = total + lax.dot_general(
                jnp.where(left, 1.0, 0.0).astype(BF16),
                jnp.concatenate([row, lane], axis=0).astype(BF16),
                (((1,), (1,)), ((), ())),
                preferred_element_type=F32,
            )
        for q in range(9):
            inv_row[q] = total[24 * q : 24 * q + 24, :128].astype(I32) - 1
            inv_lane[q] = total[24 * q : 24 * q + 24, 128:].astype(I32)
        inv_row[9, 0:16] = total[216:232, :128].astype(I32) - 1
        inv_lane[9, 0:16] = total[216:232, 128:].astype(I32)

        for j in range(3):
            loads[2 + j].wait()
        y0[...] = jnp.zeros(y0.shape, F32)
        group = lax.broadcasted_iota(I32, (32, 128), 1) >> 4
        firsts = []
        for k in range(3):
            for j in range(3):
                y0[j, 0:NCHUNK] = ginv[j, pl.ds(k, NCHUNK, stride=WIDTH), :]
            firsts.append(permuted())
        pairs = []
        cpad[...] = jnp.zeros(cpad.shape, F32)
        for kb in range(9):
            cpad[0:WELLS, 0:NCHUNK] = couple[kb]
            pairs.append(lane_pick(cpad[...].T[0:32], group)[:NCHUNK])
        for a in range(3):
            for b in range(3):
                total = firsts[0][a][:NCHUNK] * pairs[b]
                for k in (1, 2):
                    total = total + firsts[k][a][:NCHUNK] * pairs[3 * k + b]
                chain[3 * a + b] = total
        for b in range(3):
            ends[b, 0:8] = jnp.zeros((8, 128), F32)

    def permuted():
        lane = lax.broadcasted_iota(I32, (8, 128), 1)
        result = []
        for a in range(3):
            source = (lane >> 4) * WIDTH + 3 * (lane & 15) + a
            tiles = [None] * 4
            for j in range(3):
                here = (source >> 7) == j
                for i in range(4):
                    value = lane_pick(y0[j, 8 * i : 8 * i + 8], source & 127)
                    tiles[i] = value if j == 0 else jnp.where(here, value, tiles[i])
            result.append(jnp.concatenate(tiles, axis=0))
        return result

    def wells(it):
        row_of = seg_row[...]
        lane_of = seg_lane[...]
        tiles = [slice(128 * i, 128 * i + 128) for i in range(3)]
        sub = lax.broadcasted_iota(I32, (8, 128), 0)
        along = lax.broadcasted_iota(I32, (8, 128), 1)
        mine = (along >> 4) == sub

        def one_row(values):
            value = lane_pick(values[:, 384:], along & 15)
            return jnp.sum(jnp.where(mine, value, 0), axis=0, keepdims=True)

        end_row = jnp.broadcast_to(one_row(row_of), (8, 128)) - sub
        end_lane = jnp.broadcast_to(one_row(lane_of), (8, 128))

        def take(q, got):
            got = list(got)
            for i, tile in enumerate(tiles):
                base = row_of[:, tile] - q * ROWS
                new = look_up(
                    lambda a, r: pool[it, q, a, r : r + 1, :],
                    lane_of[:, tile],
                    ROWS,
                    base,
                    got[3 * i : 3 * i + 3],
                )
                got[3 * i : 3 * i + 3] = new
            base = end_row - q * ROWS
            for r in range(0, 24, 8):
                match = base == r
                for a in range(3):
                    value = lane_pick(pool[it, q, a, r : r + 8, :], end_lane)
                    got[9 + a] = jnp.where(match, value, got[9 + a])
            match = (base == 24) & (sub == 0)
            for a in range(3):
                value = lane_pick(pool[it, q, a, 24:25, :], end_lane)
                got[9 + a] = jnp.where(match, value, got[9 + a])
            return tuple(got)

        def step(p, got):
            low, high = pair(p)
            for side in (low, high):

                @pl.when(exists_at(side) & (p > 0))
                def _(side=side):
                    fwd_arrival(it, side).wait_recv()

            return take(high, take(low, got))

        none = jnp.zeros((WELLS, 128), F32)
        got = take(4, tuple([none] * 12))
        for side in range(2):

            @pl.when(exists(3 + 2 * side))
            def _(side=side):
                fwd_arrival(it, 3 + 2 * side).wait_recv()
                fwd_relay(it, side).start()

        got = list(lax.fori_loop(0, 4, step, got))
        for a in range(3):
            value = jnp.sum(got[9 + a], axis=0, keepdims=True)
            value = lane_pick(value, (sub * 16 + along) & 127)
            got[9 + a] = jnp.where(along < 16, value, 0.0)
        none = jnp.zeros((WELLS, 128), F32)
        for i in range(4):
            square = jnp.concatenate([got[3 * i + a] for a in range(3)] + [none] * 13, axis=0)
            spread[128 * i : 128 * i + 128] = square.T
        well = [(along + 128 * j) // WIDTH for j in range(3)]
        for j in range(3):
            totals = [None] * NCHUNK
            for a in range(3):
                for c in range(NCHUNK):
                    for at in (SPAN * c, SPAN * c + 8):
                        r = lane_pick(spread[at : at + 8], well[j] + 8 * a)
                        g = ginv[j, pl.ds(3 * at + a, 8, stride=3), :]
                        totals[c] = g * r if totals[c] is None else totals[c] + g * r
            for c in range(NCHUNK):
                y0[j, c : c + 1, :] = jnp.sum(totals[c], axis=0, keepdims=True)
        moved = permuted()
        for a in range(3):
            yp[a] = moved[a]

        def link(c, last):
            new = []
            for a in range(3):
                value = yp[a, pl.ds(c, 1), :]
                for b in range(3):
                    value = value - chain[3 * a + b, pl.ds(c, 1), :] * last[b]
                new.append(value)
            for a in range(3):
                ends[a, pl.ds(c + 1, 1), :] = new[a]
            return tuple(new)

        lax.fori_loop(0, NCHUNK, link, tuple([jnp.zeros((1, 128), F32)] * 3), unroll=5)
        last_lane = lax.broadcasted_iota(I32, (NCHUNK, 128), 1) | 15
        before = [lane_pick(ends[b, 0:NCHUNK, :], last_lane) for b in range(3)]
        for a in range(3):
            value = yp[a, 0:NCHUNK]
            for b in range(3):
                value = value - chain[3 * a + b] * before[b]
            ytab[a] = value

        def corrections(row_at, lane_at):
            return look_up(lambda a, r: ytab[a, r : r + 1, :], lane_at, ROWS, row_at)

        for half in range(2):
            tile = slice(8 * half, 8 * half + 8)
            got = corrections(inv_row[9, tile], inv_lane[9, tile])
            for q in range(8 * half, min(9, 8 * half + 8)):
                for a in range(3):
                    slots[it, q, a, 24:25] = got[a][q - 8 * half : q - 8 * half + 1]

        def give(q):
            for i in range(3):
                tile = slice(8 * i, 8 * i + 8)
                got = corrections(inv_row[q, tile], inv_lane[q, tile])
                for a in range(3):
                    slots[it, q, a, tile] = got[a]

        def give_pair(t, carry):
            kind = jnp.where(t == 2, 0, jnp.where(t == 3, 1, 3 - t))
            for side, q in enumerate(pair(kind)):
                give(q)

            for side, q in enumerate(pair(kind)):

                @pl.when(exists_at(q) & (t == 0))
                def _(side=side):
                    back_relay(it, side).start()

                @pl.when(exists_at(q) & (t == 2))
                def _(side=side):
                    back_relay(it, side).wait_recv()
                    here = slots[it, 3 + 2 * side] + relay[it, side]
                    slots[it, 3 + 2 * side] = here

                @pl.when(exists_at(q) & (t > 0))
                def _(q=q):
                    back_copy(it, q).start()

            return carry

        lax.fori_loop(0, 4, give_pair, 0)
        give(4)

    def backward(it):
        ret[...] = slots[it, 4]
        for q in ORDER:

            @pl.when(direct(q))
            def _(q=q):
                back_copy(it, 8 - q).wait_recv()
                ret[...] = ret[...] + back[it, q]

        def plane(x):
            for i in range(2):
                sides = []
                for half in range(2):
                    tile = (slice(8 * i, 8 * i + 8), slice(128 * half, 128 * half + 128))
                    row_at = cell_row[(x,) + tile]
                    lane_at = cell_lane[(x,) + tile]
                    got = look_up(lambda a, r: ret[a, r : r + 1, :], lane_at, ROWS, row_at)
                    for a in range(3):
                        value = got[a]
                        for b in range(3):
                            value = value + cinv[(3 * a + b, x) + tile] * field[(it, b, x) + tile]
                        zp[(it, x + 1, a) + tile] = value
                        if i == 0:
                            ystage[it, 0, x, a : a + 1, tile[1]] = value[0:1]
                        else:
                            ystage[it, 1, x, a : a + 1, tile[1]] = value[7:8]

        def planes(t, carry):
            plane(t)
            plane(3 - t)

            @pl.when((t == 0) & exists(1))
            def _():
                halo_copy(it, 0).start()

            @pl.when((t == 0) & exists(7))
            def _():
                halo_copy(it, 1).start()

            return carry

        lax.fori_loop(0, 2, planes, 0)
        start_halo(it, 2)
        start_halo(it, 3)

    def start_halo(it, side):
        @pl.when(exists(side_place[side]))
        def _():
            halo_copy(it, side).start()

    def jacobian(it, between=lambda: None):
        row = lax.broadcasted_iota(I32, (CY, CZ), 0)
        column = lax.broadcasted_iota(I32, (CY, CZ), 1)
        for x in range(CX):
            total = [None] * 3

            def add(blocks, value, b):
                for a in range(3):
                    term = blocks(3 * a + b) * value
                    total[a] = term if total[a] is None else total[a] + term

            for b in range(3):
                here = zp[it, x + 1, b]
                add(lambda e: diag[e, x], here, b)
                if x > 0:
                    add(lambda e: off[0, e, x], zp[it, x, b], b)
                if x < CX - 1:
                    add(lambda e: off[1, e, x], zp[it, x + 2, b], b)
                value = jnp.where(row > 0, pltpu.roll(here, 1, 0), 0.0)
                add(lambda e: off[2, e, x], value, b)
                value = jnp.where(row < CY - 1, pltpu.roll(here, CY - 1, 0), 0.0)
                add(lambda e: off[3, e, x], value, b)
                value = jnp.where(column > 0, pltpu.roll(here, 1, 1), 0.0)
                add(lambda e: off[4, e, x], value, b)
                value = jnp.where(column < CZ - 1, pltpu.roll(here, CZ - 1, 1), 0.0)
                add(lambda e: off[5, e, x], value, b)
            for a in range(3):
                field[it + 1, a, x] = total[a]

        result = between()
        for side in range(4):

            @pl.when(exists(side_place[side]))
            def _(side=side):
                halo_copy(it, side ^ 1).wait_recv()
                if side < 2:
                    x = 0 if side == 0 else CX - 1
                    plane = 0 if side == 0 else CX + 1
                    for a in range(3):
                        value = field[it + 1, a, x]
                        for b in range(3):
                            value = value + off[side, 3 * a + b, x] * zp[it, plane, b]
                        field[it + 1, a, x] = value
                else:
                    y = 0 if side == 2 else CY - 1
                    for x in range(CX):
                        for a in range(3):
                            value = field[it + 1, a, x, y : y + 1, :]
                            for b in range(3):
                                beside = yhalo[it, side - 2, x, b : b + 1, :]
                                value = value + off[side, 3 * a + b, x, y : y + 1, :] * beside
                            field[it + 1, a, x, y : y + 1, :] = value
        return result

    def dot_row(place, first, second):
        total = None
        for a in range(3):
            for x in range(CX):
                product = first(a, x) * second(a, x)
                total = product if total is None else total + product
        total = jnp.sum(total, axis=0, keepdims=True)
        sums[place : place + 1, :] = total[:, :128] + total[:, 128:]

    def pack_sums(i):
        sub = lax.broadcasted_iota(I32, (8, 128), 0)
        along = lax.broadcasted_iota(I32, (8, 128), 1)
        total = jnp.sum(sums[...], axis=1, keepdims=True)
        ar1[i, 0] = jnp.sum(jnp.where(sub == along, total, 0.0), axis=0, keepdims=True)

    sums[...] = jnp.zeros((8, 128), F32)

    r_of = lambda a, x: rhs[a, x]
    w1_of = lambda a, x: field[1, a, x]
    w2_of = lambda a, x: field[2, a, x]
    v2_of = lambda a, x: field[0, a, x]

    forward(0)
    pl.semaphore_wait(barrier, greeted)
    send_forward(0)
    setup()
    wells(0)
    sent(0, fwd_copy, 9)
    loads[0].wait()
    backward(0)
    loads[1].wait()
    jacobian(0)
    forward(1)
    send_forward(1)
    dot_row(0, r_of, r_of)
    dot_row(1, w1_of, r_of)
    pack_sums(0)
    send_near(0)
    sent(0, back_copy, 9)
    sent_halo(0)
    wells(1)
    pass_on(0)
    sent(1, fwd_copy, 9)
    backward(1)

    def between():
        first = collect(0)
        square = first[:, 0:1]
        along = first[:, 1:2] / square
        for a in range(3):
            for x in range(CX):
                field[0, a, x] = field[1, a, x] - along * rhs[a, x]
        dot_row(0, v2_of, v2_of)
        dot_row(4, v2_of, r_of)
        return square, along

    square, along = jacobian(1, between)
    for a in range(3):
        for x in range(CX):
            field[2, a, x] = field[2, a, x] - along * field[1, a, x]
    dot_row(1, w2_of, r_of)
    dot_row(2, w2_of, v2_of)
    dot_row(3, w2_of, w2_of)
    pack_sums(1)
    send_near(1)
    stores = [
        pltpu.make_async_copy(zp.at[:, 1 : CX + 1], z_out, load_sem.at[0]),
        pltpu.make_async_copy(field.at[1:3], w_out, load_sem.at[1]),
    ]
    for store in stores:
        store.start()
    sent(1, back_copy, 9)
    sent_halo(1)
    sent_sums(0)
    pass_on(1)
    second = collect(1)

    beta = jnp.sqrt(square)
    size = jnp.sqrt(second[:, 0:1])
    top_first = along
    sub_first = size / beta
    top_second = second[:, 1:2] / (size * beta)
    mid_second = second[:, 2:3] / (size * size) - top_second * (second[:, 4:5] / (size * beta))
    gram_first = top_first * top_first + sub_first * sub_first
    gram_cross = top_first * top_second + sub_first * mid_second
    gram_second = second[:, 3:4] / (size * size)
    determinant = gram_first * gram_second - gram_cross * gram_cross
    weight_one = (gram_second * beta * top_first - gram_cross * beta * top_second) / determinant
    weight_two = (gram_first * beta * top_second - gram_cross * beta * top_first) / determinant
    one = weight_one / beta
    two = weight_two / size
    mixed = one - two * along
    along_lanes = lax.broadcasted_iota(I32, (1, 128), 1)
    weights[...] = jnp.where(along_lanes == 0, mixed, jnp.where(along_lanes == 1, two, one))
    for store in stores:
        store.wait()
    sent_sums(1)


def combine(rhs, z, w, weights, sol, res):
    mixed, two, one = weights[:, 0:1], weights[:, 1:2], weights[:, 2:3]
    for a in range(3):
        for x in range(CX):
            sol[a, x] = mixed * z[0, x, a] + two * z[1, x, a]
            res[a, x] = rhs[a, x] - one * w[0, a, x] - two * w[1, a, x]


def body(
    right_side,
    diag_blocks,
    off_blocks,
    cell_inverse,
    send_cells,
    recv_index,
    seg_count,
    span_inverse,
    span_couple,
):
    n_gx, n_gy = lax.axis_size("gx"), lax.axis_size("gy")
    vmem = pl.BlockSpec(memory_space=pltpu.VMEM)
    anywhere = pl.BlockSpec(memory_space=pl.ANY)
    smem = pl.BlockSpec(memory_space=pltpu.SMEM)
    dma = pltpu.SemaphoreType.DMA
    scratch = [
        pltpu.VMEM((6, 9, CX, CY, CZ), F32),
        pltpu.VMEM((9, CX, CY, CZ), F32),
        pltpu.VMEM((3, NCHUNK * WIDTH, 128), F32),
        pltpu.VMEM((3, 3, CX, CY, CZ), F32),
        pltpu.VMEM((3, 2, CX, CY, 128), F32),
        pltpu.VMEM((2, CX + 2, 3, CY, CZ), F32),
        pltpu.VMEM((2, 2, CX, 3, CZ), F32),
        pltpu.VMEM((2, 2, CX, 3, CZ), F32),
        pltpu.VMEM((2, 9, 3, ROWS, 128), F32),
        pltpu.VMEM((2, 9, 3, ROWS, 128), F32),
        pltpu.VMEM((2, 9, 3, ROWS, 128), F32),
        pltpu.VMEM((2, 2, 3, ROWS, 128), F32),
        pltpu.VMEM((3, ROWS, 128), F32),
        pltpu.VMEM((ROWS, 128), I32),
        pltpu.VMEM((WELLS, 512), I32),
        pltpu.VMEM((WELLS, 512), I32),
        pltpu.VMEM((10, 24, 128), I32),
        pltpu.VMEM((10, 24, 128), I32),
        pltpu.VMEM((CX, CY, CZ), I32),
        pltpu.VMEM((CX, CY, CZ), I32),
        pltpu.VMEM((512, 128), F32),
        pltpu.VMEM((3, 32, 128), F32),
        pltpu.VMEM((3, 32, 128), F32),
        pltpu.VMEM((9, NCHUNK, 128), F32),
        pltpu.VMEM((3, 32, 128), F32),
        pltpu.VMEM((3, NCHUNK, 128), F32),
        pltpu.VMEM((128, 128), F32),
        pltpu.VMEM((2, 2 * n_gy, 1, 128), F32),
        pltpu.VMEM((2, n_gx // 2, 1, 128), F32),
        pltpu.VMEM((8, 128), F32),
        dma((5,)),
        dma((2, 9)),
        dma((2, 9)),
        dma((2, 9)),
        dma((2, 9)),
        dma((2, 2)),
        dma((2, 4)),
        dma((2, 4)),
        dma((2, 2 * n_gy)),
        dma((2, 2 * n_gy)),
        dma((2, n_gx // 2)),
        dma((2, n_gx // 2)),
    ]
    z, w, weights = pl.pallas_call(
        functools.partial(kernel, n_gx, n_gy),
        out_shape=(
            jax.ShapeDtypeStruct((2, CX, 3, CY, CZ), F32),
            jax.ShapeDtypeStruct((2, 3, CX, CY, CZ), F32),
            jax.ShapeDtypeStruct((1, 128), F32),
        ),
        in_specs=[vmem, vmem, anywhere, anywhere, vmem, vmem, smem, anywhere, vmem],
        out_specs=(anywhere, anywhere, vmem),
        scratch_shapes=scratch,
        compiler_params=pltpu.CompilerParams(collective_id=0, has_side_effects=True),
        name="gmres",
    )(
        right_side,
        diag_blocks,
        off_blocks,
        cell_inverse,
        send_cells,
        recv_index,
        seg_count,
        span_inverse.reshape(NCHUNK * WIDTH, LANES),
        span_couple.transpose(1, 2, 0),
    )
    shape = jax.ShapeDtypeStruct(right_side.shape, F32)
    return pl.pallas_call(
        combine,
        out_shape=(shape, shape),
        in_specs=[vmem] * 4,
        out_specs=(vmem, vmem),
        name="combine",
    )(right_side, z, w, weights)


def solution(mesh):
    return jax.shard_map(
        body,
        mesh=mesh,
        in_specs=(
            P(None, "gx", "gy", None),
            P(None, "gx", "gy", None),
            P(None, None, "gx", "gy", None),
            P(None, "gx", "gy", None),
            P(("gx", "gy"), None),
            P(("gx", "gy"), None),
            P(("gx", "gy")),
            P(None, None, ("gx", "gy")),
            P(None, None, ("gx", "gy")),
        ),
        out_specs=(P(None, "gx", "gy", None), P(None, "gx", "gy", None)),
        check_vma=False,
    )
```

```python
import functools

import jax
import jax.numpy as jnp
from jax import lax
from jax.experimental import pallas as pl
from jax.experimental.pallas import tpu as pltpu
from jax.sharding import PartitionSpec as P

CX, CY, CZ = 4, 16, 256
WELLS = 8
MAXSEG = 400
SPAN = 16
NCHUNK = 25
WIDTH = 3 * SPAN
LANES = WELLS * WIDTH
ROWS = 25
MESH = pl.DeviceIdType.MESH
F32, BF16, I32 = jnp.float32, jnp.bfloat16, jnp.int32
NEAR = [(a, b) for a in (-1, 0, 1) for b in (-1, 0, 1)]
ORDER = [7, 1, 3, 5, 6, 8, 0, 2]


def lane_pick(row, lane):
    numbers = lax.GatherDimensionNumbers(
        offset_dims=(),
        collapsed_slice_dims=(1,),
        start_index_map=(1,),
        operand_batching_dims=(0,),
        start_indices_batching_dims=(0,),
    )
    return lax.gather(
        jnp.broadcast_to(row, lane.shape),
        lane[..., None],
        numbers,
        slice_sizes=(1, 1),
        mode=lax.GatherScatterMode.PROMISE_IN_BOUNDS,
    )


def look_up(rows, lane, count, row_at, old=None):
    levels = (count - 1).bit_length()
    bits = [(row_at & (1 << b)) != 0 for b in range(levels)]
    inside = (row_at >= 0) & (row_at < count)

    def tree(a, low, level):
        if level == 0:
            return lane_pick(rows(a, low), lane)
        left = tree(a, low, level - 1)
        if low + (1 << level - 1) >= count:
            return left
        return jnp.where(bits[level - 1], tree(a, low + (1 << level - 1), level - 1), left)

    return [
        jnp.where(inside, tree(a, 0, levels), 0.0 if old is None else old[a]) for a in range(3)
    ]


def kernel(
    n_gx,
    n_gy,
    rhs_hbm,
    diag_hbm,
    off_hbm,
    cinv_hbm,
    send_hbm,
    recv_hbm,
    seg_count_hbm,
    ginv_hbm,
    couple_hbm,
    z_out,
    w_out,
    weights,
    off,
    cinv,
    ginv,
    field,
    u,
    zp,
    ystage,
    yhalo,
    pool,
    slots,
    back,
    relay,
    ret,
    cell,
    seg_row,
    seg_lane,
    inv_row,
    inv_lane,
    cell_row,
    cell_lane,
    spread,
    y0,
    yp,
    chain,
    ends,
    ytab,
    cpad,
    ar1,
    ar2,
    sums,
    rhs,
    diag,
    send,
    recv,
    seg_count,
    couple,
    load_sem,
    fwd_send,
    fwd_recv,
    back_send,
    back_recv,
    relay_recv,
    halo_send,
    halo_recv,
    ar1_send,
    ar1_recv,
    ar2_send,
    ar2_recv,
):
    ix = lax.axis_index("gx")
    iy = lax.axis_index("gy")
    core = lax.rem(ix, 2)
    chip = lax.div(ix, 2)
    chips = n_gx // 2
    near = 2 * n_gy

    loads = [
        pltpu.make_async_copy(cinv_hbm, cinv, load_sem.at[0]),
        pltpu.make_async_copy(off_hbm, off, load_sem.at[1]),
    ] + [
        pltpu.make_async_copy(
            ginv_hbm.at[:, j * 128 : j * 128 + 128], ginv.at[j], load_sem.at[2 + j]
        )
        for j in range(3)
    ]
    early = [
        pltpu.make_async_copy(source, goal, load_sem.at[5 + i])
        for i, (source, goal) in enumerate(
            [
                (rhs_hbm, rhs),
                (diag_hbm, diag),
                (send_hbm, send),
                (recv_hbm, recv),
                (seg_count_hbm, seg_count),
                (couple_hbm, couple),
            ]
        )
    ]
    for load in early + loads:
        load.start()

    def exists(q):
        a, b = NEAR[q]
        good = True
        if a < 0:
            good = ix > 0
        elif a > 0:
            good = ix < n_gx - 1
        if b < 0:
            good = good & (iy > 0)
        elif b > 0:
            good = good & (iy < n_gy - 1)
        return good

    def device(q):
        if isinstance(q, int):
            return (ix + NEAR[q][0], iy + NEAR[q][1])
        return (ix + lax.div(q, 3) - 1, iy + lax.rem(q, 3) - 1)

    def exists_at(q):
        gx, gy = device(q)
        return (gx >= 0) & (gx < n_gx) & (gy >= 0) & (gy < n_gy) & (q != 4)

    partner = 1 - 2 * core

    def direct(q):
        a, b = NEAR[q]
        return exists(q) & (partner != a) if a and b else exists(q)

    def pair(kind):
        middle = 4 + 3 * partner * jnp.where(kind == 3, 1, jnp.where(kind == 2, -1, 0))
        reach = jnp.where(kind == 1, 3, 1)
        return (middle - reach, middle + reach)

    def near_device(d):
        place = lax.rem(core * n_gy + iy + d, near)
        return (chip * 2 + lax.div(place, n_gy), lax.rem(place, n_gy))

    def far_device(d):
        return (lax.rem(chip + d, chips) * 2 + core, iy)

    barrier = pltpu.get_barrier_semaphore()
    for q in ORDER:

        @pl.when(exists(q))
        def _(q=q):
            pl.semaphore_signal(barrier, inc=1, device_id=device(q), device_id_type=MESH)

    for d in range(1, near):
        pl.semaphore_signal(barrier, inc=1, device_id=near_device(d), device_id_type=MESH)
    for d in range(1, chips):
        pl.semaphore_signal(barrier, inc=1, device_id=far_device(d), device_id_type=MESH)

    def present(edge):
        return jnp.where(edge, 1, 0)

    across_x = 1 + present(ix > 0) + present(ix < n_gx - 1)
    across_y = 1 + present(iy > 0) + present(iy < n_gy - 1)
    greeted = across_x * across_y - 1 + (near - 1) + (chips - 1)

    def fwd_copy(it, q):
        return pltpu.make_async_remote_copy(
            src_ref=pool.at[it, 4],
            dst_ref=pool.at[it, 8 - q],
            send_sem=fwd_send.at[it, q],
            recv_sem=fwd_recv.at[it, 8 - q],
            device_id=device(q),
            device_id_type=MESH,
        )

    def fwd_arrival(it, q):
        return pltpu.make_async_remote_copy(
            src_ref=pool.at[it, 4],
            dst_ref=pool.at[it, q],
            send_sem=fwd_send.at[it, 8 - q],
            recv_sem=fwd_recv.at[it, q],
            device_id=device(q),
            device_id_type=MESH,
        )

    def fwd_relay(it, side):
        b = 2 * side - 1
        return pltpu.make_async_remote_copy(
            src_ref=pool.at[it, 4 + b],
            dst_ref=pool.at[it, 4 - 3 * partner + b],
            send_sem=fwd_send.at[it, 4 + 3 * partner + b],
            recv_sem=fwd_recv.at[it, 4 - 3 * partner + b],
            device_id=(ix + partner, iy),
            device_id_type=MESH,
        )

    def back_relay(it, side):
        q = 4 + 3 * partner + 2 * side - 1
        return pltpu.make_async_remote_copy(
            src_ref=slots.at[it, q],
            dst_ref=relay.at[it, side],
            send_sem=back_send.at[it, q],
            recv_sem=relay_recv.at[it, side],
            device_id=(ix + partner, iy),
            device_id_type=MESH,
        )

    def back_copy(it, q):
        return pltpu.make_async_remote_copy(
            src_ref=slots.at[it, q],
            dst_ref=back.at[it, 8 - q],
            send_sem=back_send.at[it, q],
            recv_sem=back_recv.at[it, 8 - q],
            device_id=device(q),
            device_id_type=MESH,
        )

    side_place = [1, 7, 3, 5]

    def halo_copy(it, side):
        if side < 2:
            src = zp.at[it, 1 if side == 0 else CX]
            dst = zp.at[it, CX + 1 if side == 0 else 0]
        else:
            src = ystage.at[it, side - 2]
            dst = yhalo.at[it, 3 - side]
        other = side ^ 1
        return pltpu.make_async_remote_copy(
            src_ref=src,
            dst_ref=dst,
            send_sem=halo_send.at[it, side],
            recv_sem=halo_recv.at[it, other],
            device_id=device(side_place[side]),
            device_id_type=MESH,
        )

    def near_copy(i, d):
        return pltpu.make_async_remote_copy(
            src_ref=ar1.at[i, 0],
            dst_ref=ar1.at[i, d],
            send_sem=ar1_send.at[i, d],
            recv_sem=ar1_recv.at[i, d],
            device_id=near_device(d),
            device_id_type=MESH,
        )

    def far_copy(i, d):
        return pltpu.make_async_remote_copy(
            src_ref=ar2.at[i, 0],
            dst_ref=ar2.at[i, d],
            send_sem=ar2_send.at[i, d],
            recv_sem=ar2_recv.at[i, d],
            device_id=far_device(d),
            device_id_type=MESH,
        )

    def sent(it, copy, count, place=lambda k: k):
        for k in range(count):
            if place(k) != 4:

                @pl.when(exists(place(k)))
                def _(k=k):
                    copy(it, k).wait_send()

    def sent_halo(it):
        sent(it, halo_copy, 4, lambda side: side_place[side])

    def sent_sums(i):
        for d in range(1, near):
            near_copy(i, d).wait_send()
        for d in range(1, chips):
            far_copy(i, d).wait_send()

    def send_near(i):
        for d in range(1, near):
            near_copy(i, d).start()

    def pass_on(i):
        total = ar1[i, 0]
        for d in range(1, near):
            near_copy(i, d).wait_recv()
            total = total + ar1[i, d]
        ar2[i, 0] = total
        for d in range(1, chips):
            far_copy(i, d).start()

    def collect(i):
        total = ar2[i, 0]
        for d in range(1, chips):
            far_copy(i, d).wait_recv()
            total = total + ar2[i, d]
        return total

    for load in early:
        load.wait()
    for c in range(ROWS):
        cell[c : c + 1, :] = send[:, c * 128 : (c + 1) * 128]

    field[0] = rhs[...]

    def forward(it):
        for a in range(3):
            total = diag[3 * a] * field[it, 0]
            total = total + diag[3 * a + 1] * field[it, 1]
            total = total + diag[3 * a + 2] * field[it, 2]
            u[a, 0] = total[:, :, :128]
            u[a, 1] = total[:, :, 128:]
        where = cell[...]
        high = where >> 7
        lane = where & 127
        sub = lax.broadcasted_iota(I32, (8, 128), 0)
        tiles = [slice(8 * i, 8 * i + 8) for i in range(3)]
        end_high = jnp.broadcast_to(high[24:25], (8, 128)) - 2 * sub
        end_lane = jnp.broadcast_to(lane[24:25], (8, 128))

        def step(g, got):
            got = list(got)
            for i, tile in enumerate(tiles):
                base = high[tile] - 64 * g
                new = look_up(
                    lambda a, r: u[a, r % 2, 2 * g + r // 32, r // 2 % 16 : r // 2 % 16 + 1, :],
                    lane[tile],
                    64,
                    base,
                    got[3 * i : 3 * i + 3],
                )
                got[3 * i : 3 * i + 3] = new
            base = end_high - 64 * g
            for r in range(0, 32, 8):
                for half in range(2):
                    match = base == 2 * r + half
                    for a in range(3):
                        here = u[a, half, 2 * g + r // 16, r % 16 : r % 16 + 8, :]
                        value = lane_pick(here, end_lane)
                        got[9 + a] = jnp.where(match, value, got[9 + a])
            return tuple(got)

        none = jnp.zeros((8, 128), F32)
        got = lax.fori_loop(0, CX // 2, step, tuple([none] * 12))
        for a in range(3):
            for i, tile in enumerate(tiles):
                pool[it, 4, a, tile] = got[3 * i + a]
            pool[it, 4, a, 24:25] = jnp.sum(got[9 + a], axis=0, keepdims=True)

    def send_forward(it):
        for q in ORDER:

            @pl.when(direct(q))
            def _(q=q):
                fwd_copy(it, q).start()

    def setup():
        total = jnp.zeros((CX * CY, 2 * CZ), F32)
        for start, width in ((0, 1024), (1024, 1024), (2048, 1024), (3072, 128)):
            where = send[:, start : start + width]
            slot = lax.broadcasted_iota(I32, (1, width), 1) + start
            left = lax.broadcasted_iota(I32, (CX * CY, width), 0) == (where >> 8)
            hit = lax.broadcasted_iota(I32, (CZ, width), 0) == (where & 255)
            row = jnp.where(hit, ((slot >> 7) + 1).astype(F32), 0.0)
            lane = jnp.where(hit, (slot & 127).astype(F32), 0.0)
            total = total + lax.dot_general(
                jnp.where(left, 1.0, 0.0).astype(BF16),
                jnp.concatenate([row, lane], axis=0).astype(BF16),
                (((1,), (1,)), ((), ())),
                preferred_element_type=F32,
            )
        cell_row[...] = total[:, :CZ].astype(I32).reshape(CX, CY, CZ) - 1
        cell_lane[...] = total[:, CZ:].astype(I32).reshape(CX, CY, CZ)

        seg_lane[...] = jnp.zeros(seg_lane.shape, I32)
        seg_lane[:, :MAXSEG] = recv[...]
        position = seg_lane[...]
        well = lax.broadcasted_iota(I32, (WELLS, 512), 0)
        segment = lax.broadcasted_iota(I32, (WELLS, 512), 1)
        count = jnp.zeros((WELLS, 512), I32)
        for w in range(WELLS):
            count = jnp.where(well == w, seg_count[w], count)
        live = (segment < count) & (segment < MAXSEG)
        high = position >> 7
        seg_row[...] = jnp.where(live, high, -1)
        seg_lane[...] = position & 127

        sub232 = lax.broadcasted_iota(I32, (232, 512), 0)
        sub128 = lax.broadcasted_iota(I32, (128, 512), 0)
        along = lax.broadcasted_iota(I32, (1, 512), 1)
        total = jnp.zeros((232, 256), F32)
        for w in range(WELLS):
            high = seg_row[w : w + 1, :]
            slab = (high * 1311) >> 15
            row_in = high - ROWS * slab
            goal = jnp.where(row_in == ROWS - 1, 9 * 24 + slab, 24 * slab + row_in)
            left = sub232 == jnp.where(high < 0, -1, goal)
            hit = sub128 == seg_lane[w : w + 1, :]
            row = jnp.where(hit, ((along >> 4) + 1).astype(F32), 0.0)
            lane = jnp.where(hit, ((along & 15) + w * SPAN).astype(F32), 0.0)
            total = total + lax.dot_general(
                jnp.where(left, 1.0, 0.0).astype(BF16),
                jnp.concatenate([row, lane], axis=0).astype(BF16),
                (((1,), (1,)), ((), ())),
                preferred_element_type=F32,
            )
        for q in range(9):
            inv_row[q] = total[24 * q : 24 * q + 24, :128].astype(I32) - 1
            inv_lane[q] = total[24 * q : 24 * q + 24, 128:].astype(I32)
        inv_row[9, 0:16] = total[216:232, :128].astype(I32) - 1
        inv_lane[9, 0:16] = total[216:232, 128:].astype(I32)

        for j in range(3):
            loads[2 + j].wait()
        y0[...] = jnp.zeros(y0.shape, F32)
        group = lax.broadcasted_iota(I32, (32, 128), 1) >> 4
        firsts = []
        for k in range(3):
            for j in range(3):
                y0[j, 0:NCHUNK] = ginv[j, pl.ds(k, NCHUNK, stride=WIDTH), :]
            firsts.append(permuted())
        pairs = []
        cpad[...] = jnp.zeros(cpad.shape, F32)
        for kb in range(9):
            cpad[0:WELLS, 0:NCHUNK] = couple[kb]
            pairs.append(lane_pick(cpad[...].T[0:32], group)[:NCHUNK])
        for a in range(3):
            for b in range(3):
                total = firsts[0][a][:NCHUNK] * pairs[b]
                for k in (1, 2):
                    total = total + firsts[k][a][:NCHUNK] * pairs[3 * k + b]
                chain[3 * a + b] = total
        for b in range(3):
            ends[b, 0:8] = jnp.zeros((8, 128), F32)

    def permuted():
        lane = lax.broadcasted_iota(I32, (8, 128), 1)
        result = []
        for a in range(3):
            source = (lane >> 4) * WIDTH + 3 * (lane & 15) + a
            tiles = [None] * 4
            for j in range(3):
                here = (source >> 7) == j
                for i in range(4):
                    value = lane_pick(y0[j, 8 * i : 8 * i + 8], source & 127)
                    tiles[i] = value if j == 0 else jnp.where(here, value, tiles[i])
            result.append(jnp.concatenate(tiles, axis=0))
        return result

    def wells(it):
        row_of = seg_row[...]
        lane_of = seg_lane[...]
        tiles = [slice(128 * i, 128 * i + 128) for i in range(3)]
        sub = lax.broadcasted_iota(I32, (8, 128), 0)
        along = lax.broadcasted_iota(I32, (8, 128), 1)
        mine = (along >> 4) == sub

        def one_row(values):
            value = lane_pick(values[:, 384:], along & 15)
            return jnp.sum(jnp.where(mine, value, 0), axis=0, keepdims=True)

        end_row = jnp.broadcast_to(one_row(row_of), (8, 128)) - sub
        end_lane = jnp.broadcast_to(one_row(lane_of), (8, 128))

        def take(q, got):
            got = list(got)
            for i, tile in enumerate(tiles):
                base = row_of[:, tile] - q * ROWS
                new = look_up(
                    lambda a, r: pool[it, q, a, r : r + 1, :],
                    lane_of[:, tile],
                    ROWS,
                    base,
                    got[3 * i : 3 * i + 3],
                )
                got[3 * i : 3 * i + 3] = new
            base = end_row - q * ROWS
            for r in range(0, 24, 8):
                match = base == r
                for a in range(3):
                    value = lane_pick(pool[it, q, a, r : r + 8, :], end_lane)
                    got[9 + a] = jnp.where(match, value, got[9 + a])
            match = (base == 24) & (sub == 0)
            for a in range(3):
                value = lane_pick(pool[it, q, a, 24:25, :], end_lane)
                got[9 + a] = jnp.where(match, value, got[9 + a])
            return tuple(got)

        def step(p, got):
            low, high = pair(p)
            for side in (low, high):

                @pl.when(exists_at(side) & (p > 0))
                def _(side=side):
                    fwd_arrival(it, side).wait_recv()

            return take(high, take(low, got))

        none = jnp.zeros((WELLS, 128), F32)
        got = take(4, tuple([none] * 12))
        for side in range(2):

            @pl.when(exists(3 + 2 * side))
            def _(side=side):
                fwd_arrival(it, 3 + 2 * side).wait_recv()
                fwd_relay(it, side).start()

        got = list(lax.fori_loop(0, 4, step, got))
        for a in range(3):
            value = jnp.sum(got[9 + a], axis=0, keepdims=True)
            value = lane_pick(value, (sub * 16 + along) & 127)
            got[9 + a] = jnp.where(along < 16, value, 0.0)
        none = jnp.zeros((WELLS, 128), F32)
        for i in range(4):
            square = jnp.concatenate([got[3 * i + a] for a in range(3)] + [none] * 13, axis=0)
            spread[128 * i : 128 * i + 128] = square.T
        well = [(along + 128 * j) // WIDTH for j in range(3)]
        for j in range(3):
            totals = [None] * NCHUNK
            for a in range(3):
                for c in range(NCHUNK):
                    for at in (SPAN * c, SPAN * c + 8):
                        r = lane_pick(spread[at : at + 8], well[j] + 8 * a)
                        g = ginv[j, pl.ds(3 * at + a, 8, stride=3), :]
                        totals[c] = g * r if totals[c] is None else totals[c] + g * r
            for c in range(NCHUNK):
                y0[j, c : c + 1, :] = jnp.sum(totals[c], axis=0, keepdims=True)
        moved = permuted()
        for a in range(3):
            yp[a] = moved[a]

        def link(c, last):
            new = []
            for a in range(3):
                value = yp[a, pl.ds(c, 1), :]
                for b in range(3):
                    value = value - chain[3 * a + b, pl.ds(c, 1), :] * last[b]
                new.append(value)
            for a in range(3):
                ends[a, pl.ds(c + 1, 1), :] = new[a]
            return tuple(new)

        lax.fori_loop(0, NCHUNK, link, tuple([jnp.zeros((1, 128), F32)] * 3), unroll=5)
        last_lane = lax.broadcasted_iota(I32, (NCHUNK, 128), 1) | 15
        before = [lane_pick(ends[b, 0:NCHUNK, :], last_lane) for b in range(3)]
        for a in range(3):
            value = yp[a, 0:NCHUNK]
            for b in range(3):
                value = value - chain[3 * a + b] * before[b]
            ytab[a] = value

        def corrections(row_at, lane_at):
            return look_up(lambda a, r: ytab[a, r : r + 1, :], lane_at, ROWS, row_at)

        for half in range(2):
            tile = slice(8 * half, 8 * half + 8)
            got = corrections(inv_row[9, tile], inv_lane[9, tile])
            for q in range(8 * half, min(9, 8 * half + 8)):
                for a in range(3):
                    slots[it, q, a, 24:25] = got[a][q - 8 * half : q - 8 * half + 1]

        def give(q):
            for i in range(3):
                tile = slice(8 * i, 8 * i + 8)
                got = corrections(inv_row[q, tile], inv_lane[q, tile])
                for a in range(3):
                    slots[it, q, a, tile] = got[a]

        def give_pair(t, carry):
            kind = jnp.where(t == 2, 0, jnp.where(t == 3, 1, 3 - t))
            for side, q in enumerate(pair(kind)):
                give(q)

            for side, q in enumerate(pair(kind)):

                @pl.when(exists_at(q) & (t == 0))
                def _(side=side):
                    back_relay(it, side).start()

                @pl.when(exists_at(q) & (t == 2))
                def _(side=side):
                    back_relay(it, side).wait_recv()
                    here = slots[it, 3 + 2 * side] + relay[it, side]
                    slots[it, 3 + 2 * side] = here

                @pl.when(exists_at(q) & (t > 0))
                def _(q=q):
                    back_copy(it, q).start()

            return carry

        lax.fori_loop(0, 4, give_pair, 0)
        give(4)

    def backward(it):
        ret[...] = slots[it, 4]
        for q in ORDER:

            @pl.when(direct(q))
            def _(q=q):
                back_copy(it, 8 - q).wait_recv()
                ret[...] = ret[...] + back[it, q]

        def plane(x):
            for i in range(2):
                sides = []
                for half in range(2):
                    tile = (slice(8 * i, 8 * i + 8), slice(128 * half, 128 * half + 128))
                    row_at = cell_row[(x,) + tile]
                    lane_at = cell_lane[(x,) + tile]
                    got = look_up(lambda a, r: ret[a, r : r + 1, :], lane_at, ROWS, row_at)
                    for a in range(3):
                        value = got[a]
                        for b in range(3):
                            value = value + cinv[(3 * a + b, x) + tile] * field[(it, b, x) + tile]
                        zp[(it, x + 1, a) + tile] = value
                        if i == 0:
                            ystage[it, 0, x, a : a + 1, tile[1]] = value[0:1]
                        else:
                            ystage[it, 1, x, a : a + 1, tile[1]] = value[7:8]

        def planes(t, carry):
            plane(t)
            plane(3 - t)

            @pl.when((t == 0) & exists(1))
            def _():
                halo_copy(it, 0).start()

            @pl.when((t == 0) & exists(7))
            def _():
                halo_copy(it, 1).start()

            return carry

        lax.fori_loop(0, 2, planes, 0)
        start_halo(it, 2)
        start_halo(it, 3)

    def start_halo(it, side):
        @pl.when(exists(side_place[side]))
        def _():
            halo_copy(it, side).start()

    def jacobian(it, between=lambda: None):
        row = lax.broadcasted_iota(I32, (CY, CZ), 0)
        column = lax.broadcasted_iota(I32, (CY, CZ), 1)
        for x in range(CX):
            total = [None] * 3

            def add(blocks, value, b):
                for a in range(3):
                    term = blocks(3 * a + b) * value
                    total[a] = term if total[a] is None else total[a] + term

            for b in range(3):
                here = zp[it, x + 1, b]
                add(lambda e: diag[e, x], here, b)
                if x > 0:
                    add(lambda e: off[0, e, x], zp[it, x, b], b)
                if x < CX - 1:
                    add(lambda e: off[1, e, x], zp[it, x + 2, b], b)
                value = jnp.where(row > 0, pltpu.roll(here, 1, 0), 0.0)
                add(lambda e: off[2, e, x], value, b)
                value = jnp.where(row < CY - 1, pltpu.roll(here, CY - 1, 0), 0.0)
                add(lambda e: off[3, e, x], value, b)
                value = jnp.where(column > 0, pltpu.roll(here, 1, 1), 0.0)
                add(lambda e: off[4, e, x], value, b)
                value = jnp.where(column < CZ - 1, pltpu.roll(here, CZ - 1, 1), 0.0)
                add(lambda e: off[5, e, x], value, b)
            for a in range(3):
                field[it + 1, a, x] = total[a]

        result = between()
        for side in range(4):

            @pl.when(exists(side_place[side]))
            def _(side=side):
                halo_copy(it, side ^ 1).wait_recv()
                if side < 2:
                    x = 0 if side == 0 else CX - 1
                    plane = 0 if side == 0 else CX + 1
                    for a in range(3):
                        value = field[it + 1, a, x]
                        for b in range(3):
                            value = value + off[side, 3 * a + b, x] * zp[it, plane, b]
                        field[it + 1, a, x] = value
                else:
                    y = 0 if side == 2 else CY - 1
                    for x in range(CX):
                        for a in range(3):
                            value = field[it + 1, a, x, y : y + 1, :]
                            for b in range(3):
                                beside = yhalo[it, side - 2, x, b : b + 1, :]
                                value = value + off[side, 3 * a + b, x, y : y + 1, :] * beside
                            field[it + 1, a, x, y : y + 1, :] = value
        return result

    def dot_row(place, first, second):
        total = None
        for a in range(3):
            for x in range(CX):
                product = first(a, x) * second(a, x)
                total = product if total is None else total + product
        total = jnp.sum(total, axis=0, keepdims=True)
        sums[place : place + 1, :] = total[:, :128] + total[:, 128:]

    def pack_sums(i):
        sub = lax.broadcasted_iota(I32, (8, 128), 0)
        along = lax.broadcasted_iota(I32, (8, 128), 1)
        total = jnp.sum(sums[...], axis=1, keepdims=True)
        ar1[i, 0] = jnp.sum(jnp.where(sub == along, total, 0.0), axis=0, keepdims=True)

    sums[...] = jnp.zeros((8, 128), F32)

    r_of = lambda a, x: rhs[a, x]
    w1_of = lambda a, x: field[1, a, x]
    w2_of = lambda a, x: field[2, a, x]
    v2_of = lambda a, x: field[0, a, x]

    forward(0)
    pl.semaphore_wait(barrier, greeted)
    send_forward(0)
    setup()
    wells(0)
    sent(0, fwd_copy, 9)
    loads[0].wait()
    backward(0)
    loads[1].wait()
    jacobian(0)
    forward(1)
    send_forward(1)
    dot_row(0, r_of, r_of)
    dot_row(1, w1_of, r_of)
    pack_sums(0)
    send_near(0)
    sent(0, back_copy, 9)
    sent_halo(0)
    wells(1)
    pass_on(0)
    sent(1, fwd_copy, 9)
    backward(1)

    def between():
        first = collect(0)
        square = first[:, 0:1]
        along = first[:, 1:2] / square
        for a in range(3):
            for x in range(CX):
                field[0, a, x] = field[1, a, x] - along * rhs[a, x]
        dot_row(0, v2_of, v2_of)
        dot_row(4, v2_of, r_of)
        return square, along

    square, along = jacobian(1, between)
    for a in range(3):
        for x in range(CX):
            field[2, a, x] = field[2, a, x] - along * field[1, a, x]
    dot_row(1, w2_of, r_of)
    dot_row(2, w2_of, v2_of)
    dot_row(3, w2_of, w2_of)
    pack_sums(1)
    send_near(1)
    stores = [
        pltpu.make_async_copy(zp.at[:, 1 : CX + 1], z_out, load_sem.at[0]),
        pltpu.make_async_copy(field.at[1:3], w_out, load_sem.at[1]),
    ]
    for store in stores:
        store.start()
    sent(1, back_copy, 9)
    sent_halo(1)
    sent_sums(0)
    pass_on(1)
    second = collect(1)

    beta = jnp.sqrt(square)
    size = jnp.sqrt(second[:, 0:1])
    top_first = along
    sub_first = size / beta
    top_second = second[:, 1:2] / (size * beta)
    mid_second = second[:, 2:3] / (size * size) - top_second * (second[:, 4:5] / (size * beta))
    gram_first = top_first * top_first + sub_first * sub_first
    gram_cross = top_first * top_second + sub_first * mid_second
    gram_second = second[:, 3:4] / (size * size)
    determinant = gram_first * gram_second - gram_cross * gram_cross
    weight_one = (gram_second * beta * top_first - gram_cross * beta * top_second) / determinant
    weight_two = (gram_first * beta * top_second - gram_cross * beta * top_first) / determinant
    one = weight_one / beta
    two = weight_two / size
    mixed = one - two * along
    along_lanes = lax.broadcasted_iota(I32, (1, 128), 1)
    weights[...] = jnp.where(along_lanes == 0, mixed, jnp.where(along_lanes == 1, two, one))
    for store in stores:
        store.wait()
    sent_sums(1)


def combine(rhs, z, w, weights, sol, res):
    mixed, two, one = weights[:, 0:1], weights[:, 1:2], weights[:, 2:3]
    for a in range(3):
        for x in range(CX):
            sol[a, x] = mixed * z[0, x, a] + two * z[1, x, a]
            res[a, x] = rhs[a, x] - one * w[0, a, x] - two * w[1, a, x]


def body(
    right_side,
    diag_blocks,
    off_blocks,
    cell_inverse,
    send_cells,
    recv_index,
    seg_count,
    span_inverse,
    span_couple,
):
    n_gx, n_gy = lax.axis_size("gx"), lax.axis_size("gy")
    vmem = pl.BlockSpec(memory_space=pltpu.VMEM)
    anywhere = pl.BlockSpec(memory_space=pl.ANY)
    dma = pltpu.SemaphoreType.DMA
    scratch = [
        pltpu.VMEM((6, 9, CX, CY, CZ), F32),
        pltpu.VMEM((9, CX, CY, CZ), F32),
        pltpu.VMEM((3, NCHUNK * WIDTH, 128), F32),
        pltpu.VMEM((3, 3, CX, CY, CZ), F32),
        pltpu.VMEM((3, 2, CX, CY, 128), F32),
        pltpu.VMEM((2, CX + 2, 3, CY, CZ), F32),
        pltpu.VMEM((2, 2, CX, 3, CZ), F32),
        pltpu.VMEM((2, 2, CX, 3, CZ), F32),
        pltpu.VMEM((2, 9, 3, ROWS, 128), F32),
        pltpu.VMEM((2, 9, 3, ROWS, 128), F32),
        pltpu.VMEM((2, 9, 3, ROWS, 128), F32),
        pltpu.VMEM((2, 2, 3, ROWS, 128), F32),
        pltpu.VMEM((3, ROWS, 128), F32),
        pltpu.VMEM((ROWS, 128), I32),
        pltpu.VMEM((WELLS, 512), I32),
        pltpu.VMEM((WELLS, 512), I32),
        pltpu.VMEM((10, 24, 128), I32),
        pltpu.VMEM((10, 24, 128), I32),
        pltpu.VMEM((CX, CY, CZ), I32),
        pltpu.VMEM((CX, CY, CZ), I32),
        pltpu.VMEM((512, 128), F32),
        pltpu.VMEM((3, 32, 128), F32),
        pltpu.VMEM((3, 32, 128), F32),
        pltpu.VMEM((9, NCHUNK, 128), F32),
        pltpu.VMEM((3, 32, 128), F32),
        pltpu.VMEM((3, NCHUNK, 128), F32),
        pltpu.VMEM((128, 128), F32),
        pltpu.VMEM((2, 2 * n_gy, 1, 128), F32),
        pltpu.VMEM((2, n_gx // 2, 1, 128), F32),
        pltpu.VMEM((8, 128), F32),
        pltpu.VMEM((3, CX, CY, CZ), F32),
        pltpu.VMEM((9, CX, CY, CZ), F32),
        pltpu.VMEM((1, 3200), I32),
        pltpu.VMEM((WELLS, MAXSEG), I32),
        pltpu.SMEM((WELLS,), I32),
        pltpu.VMEM((9, WELLS, NCHUNK), F32),
        dma((11,)),
        dma((2, 9)),
        dma((2, 9)),
        dma((2, 9)),
        dma((2, 9)),
        dma((2, 2)),
        dma((2, 4)),
        dma((2, 4)),
        dma((2, 2 * n_gy)),
        dma((2, 2 * n_gy)),
        dma((2, n_gx // 2)),
        dma((2, n_gx // 2)),
    ]
    z, w, weights = pl.pallas_call(
        functools.partial(kernel, n_gx, n_gy),
        out_shape=(
            jax.ShapeDtypeStruct((2, CX, 3, CY, CZ), F32),
            jax.ShapeDtypeStruct((2, 3, CX, CY, CZ), F32),
            jax.ShapeDtypeStruct((1, 128), F32),
        ),
        in_specs=[anywhere] * 9,
        out_specs=(anywhere, anywhere, vmem),
        scratch_shapes=scratch,
        compiler_params=pltpu.CompilerParams(collective_id=0, has_side_effects=True),
        name="gmres",
    )(
        right_side,
        diag_blocks,
        off_blocks,
        cell_inverse,
        send_cells,
        recv_index,
        seg_count,
        span_inverse.reshape(NCHUNK * WIDTH, LANES),
        span_couple.transpose(1, 2, 0),
    )
    shape = jax.ShapeDtypeStruct(right_side.shape, F32)
    return pl.pallas_call(
        combine,
        out_shape=(shape, shape),
        in_specs=[vmem] * 4,
        out_specs=(vmem, vmem),
        name="combine",
    )(right_side, z, w, weights)


def solution(mesh):
    return jax.shard_map(
        body,
        mesh=mesh,
        in_specs=(
            P(None, "gx", "gy", None),
            P(None, "gx", "gy", None),
            P(None, None, "gx", "gy", None),
            P(None, "gx", "gy", None),
            P(("gx", "gy"), None),
            P(("gx", "gy"), None),
            P(("gx", "gy")),
            P(None, None, ("gx", "gy")),
            P(None, None, ("gx", "gy")),
        ),
        out_specs=(P(None, "gx", "gy", None), P(None, "gx", "gy", None)),
        check_vma=False,
    )
```
